32 devices in a mesh: grp: 2 (over y), gx: 4 (over z), gy: 2 (over x), col: 2 (over core).
Axes of the slice: x: 2, y: 2, z: 4, core: 2. Of those that a mesh axis runs over, the one named last changes fastest.
Arguments:
- field: bfloat16 [64, 32, 32, 128], P('grp', 'gx', ('gy', 'col')), parts along dimension 0, may hold values from -6 to 6
- cotangent: bfloat16 [64, 32, 32, 128], P('grp', 'gx', ('gy', 'col')), parts along dimension 0, may hold values from -6 to 6
- mode_weight: bfloat16 [2, 32, 32, 32, 32, 32], P(None, None, None, ('gy', 'col'), 'gx'), may hold values from -3 to 3
- skip_weight: bfloat16 [32, 32], replicated, may hold values from -1 to 1
- lift_weight: bfloat16 [128, 32], replicated, may hold values from -1 to 1
- proj_weight: bfloat16 [32, 128], replicated, may hold values from -0.5 to 0.5
Outputs:
- field_grad: bfloat16 [64, 32, 32, 128], P('grp', 'gx', ('gy', 'col')), parts along dimension 0
- mode_grad: bfloat16 [4, 32, 32, 32, 32, 32], P('grp', None, None, ('gy', 'col'), 'gx'), parts along dimension 0
- skip_grad: float32 [64, 32], P('grp'), parts along dimension 0
- lift_grad: float32 [256, 32], P('grp'), parts along dimension 0
- proj_grad: float32 [64, 128], P('grp'), parts along dimension 0
The draws below stay inside these ranges and needn't reach their ends.
There are 2 independent parts, one for each index of `grp`. The reference program is written for one: setup_inputs(seed, part) draws one part's arguments, and reference() takes and returns one part's arrays. A program takes and returns all parts, laid end to end along the dimension named above; an argument that names none is the same for every part. Nothing has to cross between parts.
All inputs are finite; a program needn't handle non-finite values.
Results may differ from the reference program's by a relative error of at most 0.023.
Values may be sent and summed in bfloat16 or wider, within the bound.
A program may use at most 192 MiB of HBM per device.

```python
import math
import jax
import jax.numpy as jnp
from jax import lax

C = 32
H = 128
MX = 32
MY = 32
MZ = 32
NZ = 128
NX = 32
NY = 32


def block_scale(own_key, shape, pieces, low, high):
    loudness, own = 1.0, jax.random.fold_in(own_key, 6)
    for axis_at, shards_of in pieces:
        steps = jnp.exp(jax.random.uniform(jax.random.fold_in(own, axis_at), (shards_of,), jnp.float32, low / len(pieces), high / len(pieces)))
        loudness = loudness * jnp.repeat(steps, shape[axis_at] // shards_of).reshape([-1 if axis == axis_at else 1 for axis in range(len(shape))])
    return loudness


def bell_draw(rng, extent, scale, most, split=(), held_as=jnp.bfloat16):
    level = block_scale(rng, extent, split, -0.22, 0.18) if split else 1.0
    values = jax.random.normal(rng, extent, jnp.float32) * scale * level
    return jnp.minimum(jnp.maximum(values, -most), most).astype(held_as)


def setup_inputs(seed: int = 0, part: int = 0) -> dict:
    key_list = jax.random.split(jax.random.key(seed), 7)
    part_keys = jax.random.split(jax.random.fold_in(key_list[6], part), 7)
    field = bell_draw(part_keys[0], (C, NX, NY, NZ), 1.0, 6.0, ((1, 4), (2, 4)))
    cotangent = bell_draw(part_keys[1], (C, NX, NY, NZ), 1.0, 6.0, ((1, 4), (2, 4)))
    mode_weight = bell_draw(key_list[2], (2, C, C, MZ, MY, MX), 0.5, 3.0, ((3, 4), (4, 4)))
    skip_weight = bell_draw(key_list[3], (C, C), C ** -0.5, 1.0)
    lift_weight = bell_draw(key_list[4], (H, C), C ** -0.5, 1.0)
    proj_weight = bell_draw(key_list[5], (C, H), H ** -0.5, 0.5)
    return {"field": field, "cotangent": cotangent, "mode_weight": mode_weight, "skip_weight": skip_weight, "lift_weight": lift_weight, "proj_weight": proj_weight}


KAPPA = 0.7978845608028654
CUBIC = 0.044715

def gelu_slope(value):
    inner = KAPPA * (value + CUBIC * value * value * value)
    tangent = jnp.tanh(inner)
    result = 0.5 * value * (1.0 + tangent)
    slope = 0.5 * (1.0 + tangent) + 0.5 * value * (1.0 - tangent * tangent) * KAPPA * (1.0 + 3.0 * CUBIC * value * value)
    return (result, slope)

def trig_pair(freqs, length):
    positions = jnp.arange(length, dtype=jnp.int32)
    turns = positions[:, None] * (freqs[None, :] % length) % length
    angle = turns.astype(jnp.float32) * (2.0 * math.pi / length)
    factor = 1.0 / math.sqrt(length)
    return (jnp.cos(angle) * factor, jnp.sin(angle) * factor)

def real_table(freqs, length):
    cosine, sine = trig_pair(freqs, length)
    return jnp.stack([cosine.T, -sine.T]).astype(jnp.bfloat16)

def complex_table(freqs, length):
    cosine, sine = trig_pair(freqs, length)
    upper = jnp.stack([cosine, -sine], axis=1)
    lower = jnp.stack([sine, cosine], axis=1)
    return jnp.stack([upper, lower]).astype(jnp.bfloat16)

def centered(count):
    return jnp.arange(count, dtype=jnp.int32) - count // 2

def as_float(value):
    return value.astype(jnp.float32)

def to_modes(values, z_table, y_table, x_table):
    first = jnp.einsum('cxyn,qkn->qckxy', as_float(values), as_float(z_table)).astype(jnp.bfloat16)
    second = jnp.einsum('pckxn,pnqj->qckjx', as_float(first), as_float(y_table)).astype(jnp.bfloat16)
    return jnp.einsum('pckjn,pnql->qckjl', as_float(second), as_float(x_table)).astype(jnp.bfloat16)

def to_grid(spec, z_table, y_table, x_table):
    first = jnp.einsum('pckjl,qnpl->qckjn', as_float(spec), as_float(x_table)).astype(jnp.bfloat16)
    second = jnp.einsum('pckjx,qnpj->qckxn', as_float(first), as_float(y_table)).astype(jnp.bfloat16)
    return jnp.einsum('pckxy,pkn->cxyn', as_float(second), as_float(z_table))

def mix(weight, modes):
    wgt = as_float(weight)
    mds = as_float(modes)
    real = jnp.einsum('iokjl,ikjl->okjl', wgt[0], mds[0]) - jnp.einsum('iokjl,ikjl->okjl', wgt[1], mds[1])
    imag = jnp.einsum('iokjl,ikjl->okjl', wgt[0], mds[1]) + jnp.einsum('iokjl,ikjl->okjl', wgt[1], mds[0])
    return jnp.stack([real, imag]).astype(jnp.bfloat16)

def reference(field, cotangent, mode_weight, skip_weight, lift_weight, proj_weight):
    z_table = real_table(jnp.arange(MZ, dtype=jnp.int32), NZ)
    y_table = complex_table(centered(MY), NY)
    x_table = complex_table(centered(MX), NX)
    modes = to_modes(field, z_table, y_table, x_table)
    spectral = to_grid(mix(mode_weight, modes), z_table, y_table, x_table)
    skip_f = as_float(skip_weight)
    lift_f = as_float(lift_weight)
    proj_f = as_float(proj_weight)

    def slab_step(carry, index):
        values = as_float(lax.dynamic_index_in_dim(field, index, 1, keepdims=False).reshape(C, -1))
        grads = as_float(lax.dynamic_index_in_dim(cotangent, index, 1, keepdims=False).reshape(C, -1))
        spec = lax.dynamic_index_in_dim(spectral, index, 1, keepdims=False).reshape(C, -1)
        pre = spec + jnp.dot(skip_f, values)
        lifted, slope_pre = gelu_slope(pre)
        lifted = lifted.astype(jnp.bfloat16)
        hidden = jnp.dot(lift_f, as_float(lifted))
        activated, slope_hid = gelu_slope(hidden)
        activated = activated.astype(jnp.bfloat16)
        hidden_grad = (jnp.dot(proj_f.T, grads) * slope_hid).astype(jnp.bfloat16)
        grad_up = grads + jnp.dot(lift_f.T, as_float(hidden_grad))
        pre_grad = (grad_up * slope_pre).astype(jnp.bfloat16)
        proj_sum = carry[0] + jnp.dot(grads, as_float(activated).T)
        lift_sum = carry[1] + jnp.dot(as_float(hidden_grad), as_float(lifted).T)
        skip_sum = carry[2] + jnp.dot(as_float(pre_grad), values.T)
        return ((proj_sum, lift_sum, skip_sum), pre_grad)
    start = (jnp.zeros((C, H), jnp.float32), jnp.zeros((H, C), jnp.float32), jnp.zeros((C, C), jnp.float32))
    sums, slabs = lax.scan(slab_step, start, jnp.arange(NX, dtype=jnp.int32))
    proj_grad, lift_grad, skip_grad = sums
    pre_grad = jnp.transpose(slabs.reshape(NX, C, NY, NZ), (1, 0, 2, 3))
    pre_modes = to_modes(pre_grad, z_table, y_table, x_table)
    mds = as_float(modes)
    prm = as_float(pre_modes)
    wgt = as_float(mode_weight)
    grad_real = jnp.einsum('ikjl,okjl->iokjl', mds[0], prm[0]) + jnp.einsum('ikjl,okjl->iokjl', mds[1], prm[1])
    grad_imag = jnp.einsum('ikjl,okjl->iokjl', mds[0], prm[1]) - jnp.einsum('ikjl,okjl->iokjl', mds[1], prm[0])
    mode_grad = jnp.stack([grad_real, grad_imag]).astype(jnp.bfloat16)
    back_real = jnp.einsum('iokjl,okjl->ikjl', wgt[0], prm[0]) + jnp.einsum('iokjl,okjl->ikjl', wgt[1], prm[1])
    back_imag = jnp.einsum('iokjl,okjl->ikjl', wgt[0], prm[1]) - jnp.einsum('iokjl,okjl->ikjl', wgt[1], prm[0])
    modes_grad = jnp.stack([back_real, back_imag]).astype(jnp.bfloat16)
    spectral_grad = to_grid(modes_grad, z_table, y_table, x_table)
    field_grad = (spectral_grad + jnp.einsum('oi,oxyn->ixyn', skip_f, as_float(pre_grad))).astype(jnp.bfloat16)
    return (field_grad, mode_grad, skip_grad, lift_grad, proj_grad)
```

```python
import functools
import math

import jax
import jax.numpy as jnp
import numpy as np
from jax import lax
from jax.experimental import pallas as pl
from jax.experimental.pallas import tpu as pltpu
from jax.sharding import PartitionSpec as P

MX = 32
MY = 32
MZ = 32


KAPPA = 0.7978845608028654
CUBIC = 0.044715


def gelu_slope(value):
    inner = KAPPA * (value + CUBIC * value * value * value)
    tangent = jnp.tanh(inner)
    result = 0.5 * value * (1.0 + tangent)
    slope = 0.5 * (1.0 + tangent) + 0.5 * value * (1.0 - tangent * tangent) * KAPPA * (
        1.0 + 3.0 * CUBIC * value * value
    )
    return (result, slope)


def trig_pair(freqs, length):
    positions = jnp.arange(length, dtype=jnp.int32)
    turns = positions[:, None] * (freqs[None, :] % length) % length
    angle = turns.astype(jnp.float32) * (2.0 * math.pi / length)
    factor = 1.0 / math.sqrt(length)
    return (jnp.cos(angle) * factor, jnp.sin(angle) * factor)


def real_table(freqs, length):
    cosine, sine = trig_pair(freqs, length)
    return jnp.stack([cosine.T, -sine.T]).astype(jnp.bfloat16)


def complex_table(freqs, length):
    cosine, sine = trig_pair(freqs, length)
    upper = jnp.stack([cosine, -sine], axis=1)
    lower = jnp.stack([sine, cosine], axis=1)
    return jnp.stack([upper, lower]).astype(jnp.bfloat16)


def centered(count):
    return jnp.arange(count, dtype=jnp.int32) - count // 2


def to_modes(values, tables):
    z_table, y_table, x_table = tables
    chans, xrows, yrows, zlen = values.shape
    first = jnp.einsum("cxyn,qkn->qkycx", values, z_table, preferred_element_type=jnp.float32)
    first = first.astype(jnp.bfloat16).reshape(2, MZ, yrows, chans * xrows)
    moved = lax.all_to_all(first, ("gy", "col"), split_axis=1, concat_axis=2, tiled=True)
    second = jnp.einsum("pkyr,pyqj->qkjr", moved, y_table, preferred_element_type=jnp.float32)
    second = second.astype(jnp.bfloat16)[:, :, :, None, :]
    crossed = lax.all_to_all(second, "gx", split_axis=2, concat_axis=3, tiled=True)
    crossed = crossed.reshape(crossed.shape[:4] + (chans, xrows))
    third = jnp.einsum("pkjgcx,pgxql->qckjl", crossed, x_table, preferred_element_type=jnp.float32)
    return third.astype(jnp.bfloat16).reshape(2, chans, -1)


def to_grid(spec, tables, shape, local_modes):
    z_table, y_table, x_table = tables
    chans, xrows, yrows, zlen = shape
    spec = spec.reshape((2, chans) + local_modes)
    first = jnp.einsum("pckjl,qgxpl->qkjgcx", spec, x_table, preferred_element_type=jnp.float32)
    first = first.astype(jnp.bfloat16)
    first = first.reshape(first.shape[:4] + (chans * xrows,))
    joined = lax.all_to_all(first, "gx", split_axis=3, concat_axis=2, tiled=True)
    joined = joined.reshape(joined.shape[:3] + (chans * xrows,))
    second = jnp.einsum("pkjr,qypj->qkyr", joined, y_table, preferred_element_type=jnp.float32)
    second = second.astype(jnp.bfloat16)
    returned = lax.all_to_all(second, ("gy", "col"), split_axis=2, concat_axis=1, tiled=True)
    grid = jnp.einsum("pkyr,pkn->ryn", returned, z_table, preferred_element_type=jnp.float32)
    return grid.reshape(chans, xrows, yrows, zlen)


def mix(weight, modes):
    real = jnp.einsum("iok,ik->ok", weight[0], modes[0], preferred_element_type=jnp.float32)
    real = real - jnp.einsum("iok,ik->ok", weight[1], modes[1], preferred_element_type=jnp.float32)
    imag = jnp.einsum("iok,ik->ok", weight[0], modes[1], preferred_element_type=jnp.float32)
    imag = imag + jnp.einsum("iok,ik->ok", weight[1], modes[0], preferred_element_type=jnp.float32)
    return jnp.stack([real, imag]).astype(jnp.bfloat16)


def on_device_plain(field, cotangent, mode_weight, skip_weight, lift_weight, proj_weight):
    chans, xrows, yrows, zlen = field.shape
    groups_x = lax.axis_size("gx")
    groups_y = lax.axis_size("gy")
    groups_c = lax.axis_size("col")
    span_x = xrows * groups_x
    span_y = yrows * groups_y * groups_c
    column = jnp.arange(MZ, dtype=jnp.int32)
    z_table = real_table(column, zlen)
    y_table = complex_table(centered(MY), span_y)
    x_table = complex_table(centered(MX), span_x).reshape(2, groups_x, xrows, 2, MX)
    tables = (z_table, y_table, x_table)
    local_modes = (mode_weight.shape[3], mode_weight.shape[4], mode_weight.shape[5])
    weight_flat = mode_weight.reshape(2, chans, chans, -1)
    modes = to_modes(field, tables)
    spectral = to_grid(mix(weight_flat, modes), tables, field.shape, local_modes).reshape(chans, -1)
    flat_field = field.reshape(chans, -1)
    flat_grad = cotangent.reshape(chans, -1)
    pre = spectral + jnp.dot(skip_weight, flat_field, preferred_element_type=jnp.float32)
    lifted, slope_pre = gelu_slope(pre)
    lifted = lifted.astype(jnp.bfloat16)
    hidden = jnp.dot(lift_weight, lifted, preferred_element_type=jnp.float32)
    activated, slope_hid = gelu_slope(hidden)
    activated = activated.astype(jnp.bfloat16)
    back_hidden = jnp.dot(proj_weight.T, flat_grad, preferred_element_type=jnp.float32)
    hidden_grad = (back_hidden * slope_hid).astype(jnp.bfloat16)
    grad_up = flat_grad.astype(jnp.float32) + jnp.dot(
        lift_weight.T, hidden_grad, preferred_element_type=jnp.float32
    )
    pre_grad = (grad_up * slope_pre).astype(jnp.bfloat16)
    proj_part = jnp.einsum("cr,hr->ch", flat_grad, activated, preferred_element_type=jnp.float32)
    lift_part = jnp.einsum("hr,cr->hc", hidden_grad, lifted, preferred_element_type=jnp.float32)
    skip_part = jnp.einsum("or,ir->oi", pre_grad, flat_field, preferred_element_type=jnp.float32)
    proj_grad, lift_grad, skip_grad = lax.psum(
        (proj_part, lift_part, skip_part), ("gx", "gy", "col")
    )
    pre_modes = to_modes(pre_grad.reshape(field.shape), tables)
    grad_real = jnp.einsum("ik,ok->iok", modes[0], pre_modes[0], preferred_element_type=jnp.float32)
    grad_real = grad_real + jnp.einsum(
        "ik,ok->iok", modes[1], pre_modes[1], preferred_element_type=jnp.float32
    )
    grad_imag = jnp.einsum("ik,ok->iok", modes[0], pre_modes[1], preferred_element_type=jnp.float32)
    grad_imag = grad_imag - jnp.einsum(
        "ik,ok->iok", modes[1], pre_modes[0], preferred_element_type=jnp.float32
    )
    mode_grad = jnp.stack([grad_real, grad_imag]).astype(jnp.bfloat16).reshape(mode_weight.shape)
    back_real = jnp.einsum(
        "iok,ok->ik", weight_flat[0], pre_modes[0], preferred_element_type=jnp.float32
    )
    back_real = back_real + jnp.einsum(
        "iok,ok->ik", weight_flat[1], pre_modes[1], preferred_element_type=jnp.float32
    )
    back_imag = jnp.einsum(
        "iok,ok->ik", weight_flat[0], pre_modes[1], preferred_element_type=jnp.float32
    )
    back_imag = back_imag - jnp.einsum(
        "iok,ok->ik", weight_flat[1], pre_modes[0], preferred_element_type=jnp.float32
    )
    modes_grad = jnp.stack([back_real, back_imag]).astype(jnp.bfloat16)
    spectral_grad = to_grid(modes_grad, tables, field.shape, local_modes).reshape(chans, -1)
    skip_back = jnp.dot(skip_weight.T, pre_grad, preferred_element_type=jnp.float32)
    field_grad = (spectral_grad + skip_back).astype(jnp.bfloat16).reshape(field.shape)
    return (field_grad, mode_grad, skip_grad, lift_grad, proj_grad)


F32 = jnp.float32
BF16 = jnp.bfloat16
LANES = 128


def np_trig(freqs, length):
    turns = (np.arange(length)[:, None] * (freqs[None, :] % length)) % length
    angle = turns.astype(np.float32) * np.float32(2.0 * math.pi / length)
    factor = np.float32(1.0 / math.sqrt(length))
    return (np.cos(angle) * factor, np.sin(angle) * factor)


def np_complex(freqs, length):
    cosine, sine = np_trig(freqs, length)
    upper = np.stack([cosine, -sine], axis=1)
    lower = np.stack([sine, cosine], axis=1)
    return np.stack([upper, lower])


def host_tables(zlen, yrows, xrows, n_z, n_y, chans, half):
    cosine, sine = np_trig(np.arange(MZ), zlen)
    z_pair = np.stack([cosine.T, -sine.T], axis=1).reshape(2 * MZ, zlen)
    y_full = np_complex(np.arange(MY) - MY // 2, yrows * n_z)
    kyb = MY // n_y
    y_six = y_full.reshape(2, n_z, yrows, 2, n_y, kyb)
    y_fwd = y_six.transpose(4, 3, 5, 1, 0, 2).reshape(2 * MY, 2 * yrows * n_z)
    y_inv = y_six.transpose(1, 0, 2, 4, 3, 5).reshape(2 * yrows * n_z, 2 * MY)
    x_full = np_complex(np.arange(MX) - MX // 2, xrows * n_y).reshape(2, n_y, xrows, 2, MX)
    x_rows = x_full.transpose(1, 0, 2, 3, 4).reshape(n_y, 2, 1, xrows, 2 * MX)
    x_rows = np.broadcast_to(x_rows, (n_y, 2, half, xrows, 2 * MX)).reshape(-1, 2 * MX)
    x_fwd = np.concatenate([x_rows, x_rows], axis=1)
    x_cols = x_full.transpose(3, 4, 1, 0, 2).reshape(2 * MX, n_y, 2, 1, xrows)
    x_inv = np.broadcast_to(x_cols, (2 * MX, n_y, 2, half, xrows)).reshape(2 * MX, -1)
    swap = np.zeros((xrows, chans, chans, xrows), np.float32)
    for cell in range(xrows):
        for chan in range(chans):
            swap[cell, chan, chan, cell] = 1.0
    swap = swap.reshape(xrows * chans, chans * xrows)
    return [
        jnp.asarray(np.ascontiguousarray(table), BF16)
        for table in (z_pair, y_fwd, y_inv, x_fwd, x_inv, swap, swap.T)
    ]


def dot(left, right, dims=((1,), (0,))):
    return lax.dot_general(left, right, (dims, ((), ())), preferred_element_type=F32)


NT = ((1,), (1,))
TN = ((0,), (0,))


def gelu_pair(value):
    square = value * value
    tangent = jnp.tanh(value * (KAPPA + (KAPPA * CUBIC) * square))
    half = 0.5 + 0.5 * tangent
    result = value * half
    slope = half + result * (1.0 - tangent) * (KAPPA + (3.0 * KAPPA * CUBIC) * square)
    return (result, slope)


def layer_kernel(
    geo, field_ref, cot_ref, weight_ref, skip_ref, lift_ref, proj_ref,
    tz_ref, tyf_ref, tyi_ref, txf_ref, txi_ref, swap_ref, back_ref,
    grad_ref, modes_ref, premodes_ref, sums_out,
    held, packed, dense, cells, cots, pgrad, kxf, kxi, spec_grid, mixed, spread,
    send_z, recv_z, send_y, recv_y, sums, sums_x, sums_z, weight_sem, own_sem, send_sem, recv_sem,
):
    n_gy, n_col, n_y, chans, xrows, yrows, kzb, kyb = geo
    n_z = n_gy * n_col
    half = LANES // xrows
    parts = chans // half
    width = chans * xrows
    my_gy, my_col, my_gx = lax.axis_index("gy"), lax.axis_index("col"), lax.axis_index("gx")
    me_z, me_y = my_gy * n_col + my_col, my_gx

    folds = LANES // MX
    fold_rows = kzb * kyb // folds
    loads = weight_sem.shape[0]
    load_chans = chans // loads

    def weight_load(index):
        span = pl.ds(index * load_chans, load_chans)
        return pltpu.make_async_copy(
            weight_ref.at[:, span], held.at[:, span], weight_sem.at[index]
        )

    for index in range(loads):
        weight_load(index).start()

    def fold(tall):
        return jnp.concatenate(
            [tall[at * fold_rows:(at + 1) * fold_rows] for at in range(folds)], axis=1
        )

    block_of = lax.broadcasted_iota(jnp.int32, (fold_rows, LANES), 1) // MX

    def shifts(tiles):
        return [
            [tile] + [pltpu.roll(tile, step * MX, 1) for step in range(1, folds)] for tile in tiles
        ]

    def swap_blocks(moved):
        swapped = []
        for lane in range(folds):
            total = moved[0][-lane % folds]
            for row in range(1, folds):
                total = jnp.where(block_of == row, moved[row][(row - lane) % folds], total)
            swapped.append(total)
        return swapped

    def pack_weight(index):
        weight_load(index).wait()
        outs = 8

        def body(block, carry):
            first = block * outs
            for chan in range(index * load_chans, (index + 1) * load_chans):
                for piece in range(2):
                    for out in range(outs):
                        packed[piece, chan, first + out] = fold(held[piece, chan, first + out])
            return carry

        lax.fori_loop(0, chans // outs, body, 0)

    def peer_z(step):
        other = lax.rem(me_z + step, n_z)
        return other, {"gy": other // n_col, "col": lax.rem(other, n_col)}

    def peer_y(step):
        other = lax.rem(me_y + step, n_y)
        return other, {"gx": other}

    barrier = pltpu.get_barrier_semaphore()
    for step in range(1, n_z):
        pl.semaphore_signal(
            barrier, inc=1, device_id=peer_z(step)[1], device_id_type=pl.DeviceIdType.MESH
        )
    for step in range(1, n_y):
        pl.semaphore_signal(
            barrier, inc=1, device_id=peer_y(step)[1], device_id_type=pl.DeviceIdType.MESH
        )

    def exchange(phase, send, recv, count, me, peer):
        copies = []
        for step in range(1, count):
            other, where = peer(step)
            copy = pltpu.make_async_remote_copy(
                src_ref=send.at[other],
                dst_ref=recv.at[me],
                send_sem=send_sem.at[phase, step],
                recv_sem=recv_sem.at[phase, step],
                device_id=where,
                device_id_type=pl.DeviceIdType.MESH,
            )
            copy.start()
            copies.append(copy)
        own = pltpu.make_async_copy(send.at[me], recv.at[me], own_sem.at[phase])
        own.start()
        copies.append(own)
        return copies

    def finish(copies):
        for copy in copies:
            copy.wait()

    def cells_first(source, target):
        for cell in range(xrows):
            rows = source[:, cell, :, :].astype(F32)
            target[:, cell] = jnp.transpose(rows, (1, 0, 2)).astype(BF16)

    def start_z(source, phase):
        planes = [
            dot(tz_ref[...], source[row].reshape(width, source.shape[-1]), NT)
            for row in range(yrows)
        ]
        turned = jnp.transpose(jnp.stack(planes), (1, 0, 2))
        turned = turned.reshape(n_z, kzb, 2 * yrows, width).astype(BF16)
        for block in range(n_z):
            send_z[phase, block] = jnp.concatenate(
                [turned[block, freq] for freq in range(kzb)], axis=1
            )
        return exchange(2 * phase, send_z.at[phase], recv_z.at[phase], n_z, me_z, peer_z)

    def turn_lanes(rows, table):
        pieces = [rows[:, freq * width:(freq + 1) * width] for freq in range(kzb)]
        turned = dot(jnp.concatenate(pieces, axis=0), table).astype(BF16)
        tall = rows.shape[0]
        return jnp.concatenate(
            [turned[freq * tall:(freq + 1) * tall] for freq in range(kzb)], axis=1
        )

    def start_y(phase):
        rows = recv_z[phase].reshape(n_z * 2 * yrows, kzb * width)
        moved = turn_lanes(dot(tyf_ref[...], rows).astype(BF16), swap_ref[...])
        send_y[phase] = moved.reshape(n_y, 2 * kyb, kzb * width)
        return exchange(2 * phase + 1, send_y.at[phase], recv_y.at[phase], n_y, me_y, peer_y)

    def reach_modes(phase, target):
        blocks = [recv_y[phase, group].astype(F32) for group in range(n_y)]
        sides = []
        for part in range(parts):
            columns = []
            for group in range(n_y):
                for piece in range(2):
                    tiles = [
                        blocks[group][
                            piece * kyb:(piece + 1) * kyb,
                            freq * width + part * LANES:freq * width + (part + 1) * LANES,
                        ]
                        for freq in range(kzb)
                    ]
                    columns.append(jnp.concatenate(tiles, axis=0).astype(BF16))
            sides.append(jnp.concatenate(columns, axis=1))
        result = dot(jnp.concatenate(sides, axis=0), kxf[...])
        for part in range(parts):
            for tile in range(half * 2 * MX // LANES):
                tiles = []
                for row in range(folds):
                    top = part * kzb * kyb + row * fold_rows
                    tiles.append(
                        result[top:top + fold_rows, tile * LANES:(tile + 1) * LANES]
                    )
                moved = shifts(tiles)
                swapped = swap_blocks(moved)
                for lane in range(folds):
                    chan, piece = divmod(tile * folds + lane, 2)
                    dense[piece, part * half + chan] = swapped[lane].astype(BF16)
                    for row in range(folds):
                        target[
                            piece, part * half + chan, row * fold_rows:(row + 1) * fold_rows, :
                        ] = moved[row][-lane % folds][:, :MX].astype(BF16)

    run = 4

    def mix(first, count):
        def body(index, carry):
            at = first + index * run
            real = [dense[0, at + step] for step in range(run)]
            imag = [dense[1, at + step] for step in range(run)]
            for out in range(chans):
                short = [None, None]
                for step in range(run):
                    w_real, w_imag = packed[0, at + step, out], packed[1, at + step, out]
                    new = (
                        w_real * real[step] - w_imag * imag[step],
                        w_real * imag[step] + w_imag * real[step],
                    )
                    for piece in range(2):
                        old = short[piece]
                        short[piece] = new[piece] if old is None else old + new[piece]
                for piece in range(2):
                    mixed[piece, out] += short[piece].astype(F32)
            return carry

        lax.fori_loop(0, count // run, body, 0)

    def mix_back(begin, count):
        outs = 4

        def body(index, carry):
            first = begin + index * outs
            total = [[None, None] for _ in range(outs)]
            short = [[None, None] for _ in range(outs)]
            for summed in range(chans):
                real, imag = dense[0, summed], dense[1, summed]
                for out in range(outs):
                    w_real, w_imag = packed[0, first + out, summed], packed[1, first + out, summed]
                    new = (w_real * real + w_imag * imag, w_real * imag - w_imag * real)
                    for piece in range(2):
                        old = short[out][piece]
                        short[out][piece] = new[piece] if old is None else old + new[piece]
                        if (summed + 1) % run == 0:
                            wide, old = short[out][piece].astype(F32), total[out][piece]
                            total[out][piece] = wide if old is None else old + wide
                            short[out][piece] = None
            for out in range(outs):
                for piece in range(2):
                    mixed[piece, first + out] = total[out][piece]
            return carry

        lax.fori_loop(0, count // outs, body, 0)

    def start_back_x(phase):
        for part in range(parts):
            for tile in range(half * 2 * MX // LANES):
                tiles = []
                for lane in range(folds):
                    chan, piece = divmod(tile * folds + lane, 2)
                    tiles.append(mixed[piece, part * half + chan])
                swapped = swap_blocks(shifts(tiles))
                for row in range(folds):
                    top = part * kzb * kyb + row * fold_rows
                    spread[top:top + fold_rows, tile * LANES:(tile + 1) * LANES] = swapped[
                        row
                    ].astype(BF16)
        both = dot(spread[...], kxi[...])
        wide = [both[part * kzb * kyb:(part + 1) * kzb * kyb] for part in range(parts)]
        for group in range(n_y):
            rows = []
            for piece in range(2):
                at = (group * 2 + piece) * LANES
                rows.append(jnp.concatenate(
                    [
                        wide[part][freq * kyb:(freq + 1) * kyb, at:at + LANES]
                        for freq in range(kzb)
                        for part in range(parts)
                    ],
                    axis=1,
                ))
            send_y[phase, group] = jnp.concatenate(rows, axis=0).astype(BF16)
        return exchange(2 * phase + 1, send_y.at[phase], recv_y.at[phase], n_y, me_y, peer_y)

    def start_back_y(phase):
        rows = recv_y[phase].reshape(n_y * 2 * kyb, kzb * width)
        moved = turn_lanes(dot(tyi_ref[...], rows).astype(BF16), back_ref[...])
        send_z[phase] = moved.reshape(n_z, 2 * yrows, kzb * width)
        return exchange(2 * phase, send_z.at[phase], recv_z.at[phase], n_z, me_z, peer_z)

    def reach_grid(phase):
        tiles = []
        for block in range(n_z):
            rows = recv_z[phase, block].astype(F32)
            for freq in range(kzb):
                for piece in range(2):
                    tiles.append(
                        rows[piece * yrows:(piece + 1) * yrows, freq * width:(freq + 1) * width]
                    )
        turned = jnp.transpose(jnp.stack(tiles), (1, 0, 2)).astype(BF16)
        for row in range(yrows):
            spec_grid[row] = dot(turned[row], tz_ref[...], TN)

    def wide_cells(ref, row):
        return jnp.concatenate([ref[row, cell] for cell in range(xrows)], axis=1)

    def wide_spec(row):
        return jnp.concatenate(
            [spec_grid[row, cell * chans:(cell + 1) * chans, :] for cell in range(xrows)], axis=1
        )

    def build_x_tables():
        tall, wide = kxf.shape
        lane = lax.broadcasted_iota(jnp.int32, (tall, LANES), 1)
        line = lax.broadcasted_iota(jnp.int32, (tall, LANES), 0)
        owner = (line // xrows) % half
        pair = txf_ref[...].astype(F32)
        per_tile = LANES // (2 * MX)
        for tile in range(wide // LANES):
            keep = owner == tile * per_tile + lane // (2 * MX)
            kxf[:, tile * LANES:(tile + 1) * LANES] = jnp.where(keep, pair, 0.0).astype(BF16)
        flat = txi_ref[...].astype(F32)
        lane_owner = (lax.broadcasted_iota(jnp.int32, flat.shape, 1) // xrows) % half
        for chan in range(half):
            kxi[chan * 2 * MX:(chan + 1) * 2 * MX, :] = jnp.where(
                lane_owner == chan, flat, 0.0
            ).astype(BF16)

    cells_first(field_ref, cells)
    pl.semaphore_wait(barrier, n_z - 1 + n_y - 1)
    going = start_z(cells, 0)
    build_x_tables()
    mixed[...] = jnp.zeros(mixed.shape, F32)
    cells_first(cot_ref, cots)
    for index in range(loads // 4):
        pack_weight(index)
    finish(going)
    going = start_y(0)
    for index in range(loads // 4, loads):
        pack_weight(index)
    finish(going)
    reach_modes(0, modes_ref)
    mix(0, chans)
    finish(start_back_x(1))
    finish(start_back_y(1))
    reach_grid(1)

    sums[...] = jnp.zeros(sums.shape, F32)

    def pointwise(row, carry):
        values = wide_cells(cells, row)
        grads = wide_cells(cots, row)
        pre = wide_spec(row) + dot(skip_ref[...], values)
        lifted, slope_pre = gelu_pair(pre)
        lifted = lifted.astype(BF16)
        hidden = dot(lift_ref[...], lifted, TN)
        activated, slope_hid = gelu_pair(hidden)
        activated = activated.astype(BF16)
        hidden_grad = (dot(proj_ref[...], grads, TN) * slope_hid).astype(BF16)
        grad_up = grads.astype(F32) + dot(lift_ref[...], hidden_grad)
        pre_grad = (grad_up * slope_pre).astype(BF16)
        sums[0:chans] += dot(grads, activated, NT)
        sums[chans:2 * chans] += dot(lifted, hidden_grad, NT)
        sums[2 * chans:, 0:chans] += dot(pre_grad, values, NT)
        zlen = cells.shape[-1]
        for cell in range(xrows):
            pgrad[row, cell] = pre_grad[:, cell * zlen:(cell + 1) * zlen]
        return carry

    lax.fori_loop(0, yrows, pointwise, 0)

    share = sums.shape[0] // n_y

    def send_sums(phase, count, me, peer, source, target):
        copies = []
        for step in range(1, count):
            other, where = peer(step)
            copy = pltpu.make_async_remote_copy(
                src_ref=source(other),
                dst_ref=target.at[me],
                send_sem=send_sem.at[phase, step],
                recv_sem=recv_sem.at[phase, step],
                device_id=where,
                device_id_type=pl.DeviceIdType.MESH,
            )
            copy.start()
            copies.append(copy)
        return copies

    def rows_of(index):
        return pl.ds(pl.multiple_of(index * share, 8), share)

    sums_x[me_y] = sums[rows_of(me_y), :]
    small = send_sums(8, n_y, me_y, peer_y, lambda other: sums.at[rows_of(other)], sums_x)
    finish(start_z(pgrad, 2))
    going = start_y(2)
    finish(small)
    sums_z[me_z] = jnp.sum(sums_x[...], axis=0)
    small = send_sums(9, n_z, me_z, peer_z, lambda other: sums_z.at[me_z], sums_z)
    finish(going)
    reach_modes(2, premodes_ref)
    finish(small)
    sums_out[me_y] = jnp.sum(sums_z[...], axis=0)
    mix_back(0, chans)
    going = start_back_x(3)
    small = send_sums(10, n_y, me_y, peer_y, lambda other: sums_out.at[me_y], sums_out)
    finish(going)
    finish(small)
    finish(start_back_y(3))
    reach_grid(3)

    def last(row, carry):
        total = wide_spec(row) + dot(skip_ref[...], wide_cells(pgrad, row), TN)
        zlen = cells.shape[-1]
        for cell in range(xrows):
            grad_ref[row, cell] = total[:, cell * zlen:(cell + 1) * zlen].astype(BF16)
        return carry

    lax.fori_loop(0, yrows, last, 0)


def outer_kernel(
    modes_ref, pre_ref, grid_ref, sums_ref, out_ref, field_ref, proj_ref, lift_ref, skip_ref
):
    chans, rows = pre_ref.shape[1], pre_ref.shape[2]

    def body(out, carry):
        for top in range(0, rows, 16):
            p_real, p_imag = pre_ref[0, out, top:top + 16], pre_ref[1, out, top:top + 16]
            for chan in range(modes_ref.shape[1]):
                m_real, m_imag = modes_ref[0, chan, top:top + 16], modes_ref[1, chan, top:top + 16]
                out_ref[0, chan, out, top:top + 16] = m_real * p_real + m_imag * p_imag
                out_ref[1, chan, out, top:top + 16] = m_real * p_imag - m_imag * p_real
        return carry

    lax.fori_loop(0, chans, body, 0)
    for cell in range(grid_ref.shape[1]):
        cells = grid_ref[:, cell].astype(F32)
        field_ref[:, cell] = jnp.transpose(cells, (1, 0, 2)).astype(BF16)
    proj_ref[...] = sums_ref[0:chans]
    lift_ref[...] = sums_ref[chans:2 * chans]
    skip_ref[...] = sums_ref[2 * chans:, 0:chans]


def finish_gradients(modes, pre_modes, grid, sums):
    _, chans, rows, lanes = modes.shape
    yrows, xrows, _, zlen = grid.shape
    steps = math.gcd(chans, xrows)
    group, cells = chans // steps, xrows // steps
    return pl.pallas_call(
        outer_kernel,
        grid=(steps,),
        in_specs=[
            pl.BlockSpec((2, group, rows, lanes), lambda step: (0, step, 0, 0)),
            pl.BlockSpec((2, chans, rows, lanes), lambda step: (0, 0, 0, 0)),
            pl.BlockSpec((yrows, cells, chans, zlen), lambda step: (0, step, 0, 0)),
            pl.BlockSpec(sums.shape, lambda step: (0, 0)),
        ],
        out_specs=[
            pl.BlockSpec((2, group, chans, rows, lanes), lambda step: (0, step, 0, 0, 0)),
            pl.BlockSpec((chans, cells, yrows, zlen), lambda step: (0, step, 0, 0)),
            pl.BlockSpec((chans, LANES), lambda step: (0, 0)),
            pl.BlockSpec((chans, LANES), lambda step: (0, 0)),
            pl.BlockSpec((chans, chans), lambda step: (0, 0)),
        ],
        out_shape=(
            jax.ShapeDtypeStruct((2, chans, chans, rows, lanes), BF16),
            jax.ShapeDtypeStruct((chans, xrows, yrows, zlen), BF16),
            jax.ShapeDtypeStruct((chans, LANES), F32),
            jax.ShapeDtypeStruct((chans, LANES), F32),
            jax.ShapeDtypeStruct((chans, chans), F32),
        ),
        compiler_params=pltpu.CompilerParams(vmem_limit_bytes=60 << 20),
        name="mode_outer",
    )(modes, pre_modes, grid, sums)


def on_device(field, cotangent, mode_weight, skip_weight, lift_weight, proj_weight):
    chans, xrows, yrows, zlen = field.shape
    kzb, kyb = mode_weight.shape[3], mode_weight.shape[4]
    n_gy, n_col, n_y = lax.axis_size("gy"), lax.axis_size("col"), lax.axis_size("gx")
    n_z = n_gy * n_col
    fits = kyb == 8 and kzb % 2 == 0 and xrows == 8 and yrows == 8 and zlen == LANES
    fits = fits and lift_weight.shape[0] == LANES and (3 * chans) % (8 * n_y) == 0 and chans % 8 == 0
    fits = fits and (kzb * kyb * MX) % (16 * LANES) == 0
    if not fits or 2 * MX * 2 != LANES or chans % (LANES // xrows):
        return on_device_plain(
            field, cotangent, mode_weight, skip_weight, lift_weight, proj_weight
        )
    half = LANES // xrows
    parts = chans // half
    rows = kzb * kyb
    width = chans * xrows
    tables = host_tables(zlen, yrows, xrows, n_z, n_y, chans, half)
    weight = mode_weight.reshape(2, chans, chans, rows, MX)
    share = 3 * chans // n_y
    vmem = pl.BlockSpec(memory_space=pltpu.VMEM)
    geo = (n_gy, n_col, n_y, chans, xrows, yrows, kzb, kyb)
    grid_shape = (yrows, xrows, chans, zlen)
    spectral = (2, chans, rows, MX)
    packed = (2, chans, rows * MX // LANES, LANES)
    outs = pl.pallas_call(
        functools.partial(layer_kernel, geo),
        out_shape=(
            jax.ShapeDtypeStruct(grid_shape, BF16),
            jax.ShapeDtypeStruct(spectral, BF16),
            jax.ShapeDtypeStruct(spectral, BF16),
            jax.ShapeDtypeStruct((n_y, share, LANES), F32),
        ),
        in_specs=[vmem, vmem, pl.BlockSpec(memory_space=pl.ANY)] + [vmem] * 10,
        out_specs=(vmem,) * 4,
        scratch_shapes=[
            pltpu.VMEM(weight.shape, BF16),
            pltpu.VMEM((2, chans, chans, rows * MX // LANES, LANES), BF16),
            pltpu.VMEM(packed, BF16),
            pltpu.VMEM(grid_shape, BF16),
            pltpu.VMEM(grid_shape, BF16),
            pltpu.VMEM(grid_shape, BF16),
            pltpu.VMEM((n_y * 2 * LANES, half * 2 * MX), BF16),
            pltpu.VMEM((half * 2 * MX, n_y * 2 * LANES), BF16),
            pltpu.VMEM((yrows, width, zlen), F32),
            pltpu.VMEM(packed, F32),
            pltpu.VMEM((parts * rows, half * 2 * MX), BF16),
            pltpu.VMEM((4, n_z, 2 * yrows, kzb * width), BF16),
            pltpu.VMEM((4, n_z, 2 * yrows, kzb * width), BF16),
            pltpu.VMEM((4, n_y, 2 * kyb, kzb * width), BF16),
            pltpu.VMEM((4, n_y, 2 * kyb, kzb * width), BF16),
            pltpu.VMEM((n_y * share, LANES), F32),
            pltpu.VMEM((n_y, share, LANES), F32),
            pltpu.VMEM((n_z, share, LANES), F32),
            pltpu.SemaphoreType.DMA((8,)),
            pltpu.SemaphoreType.DMA((8,)),
            pltpu.SemaphoreType.DMA((11, max(n_z, n_y))),
            pltpu.SemaphoreType.DMA((11, max(n_z, n_y))),
        ],
        compiler_params=pltpu.CompilerParams(
            collective_id=0, has_side_effects=True, vmem_limit_bytes=60 << 20
        ),
        name="spectral_layer",
    )(field, cotangent, weight, skip_weight, lift_weight.T, proj_weight, *tables)
    grad, modes, pre_modes, sums = outs
    mode_grad, field_grad, proj_grad, lift_turned, skip_grad = finish_gradients(
        modes, pre_modes, grad, sums.reshape(3 * chans, LANES)
    )
    return (field_grad, mode_grad.reshape(mode_weight.shape), skip_grad, lift_turned.T, proj_grad)


def solution(mesh):
    in_specs = (
        P("grp", "gx", ("gy", "col"), None),
        P("grp", "gx", ("gy", "col"), None),
        P(None, None, None, ("gy", "col"), "gx", None),
        P(),
        P(),
        P(),
    )
    out_specs = (
        P("grp", "gx", ("gy", "col"), None),
        P("grp", None, None, ("gy", "col"), "gx", None),
        P("grp", None),
        P("grp", None),
        P("grp", None),
    )
    return jax.shard_map(
        on_device, mesh=mesh, in_specs=in_specs, out_specs=out_specs, check_vma=False
    )
```

```python
import functools
import math

import jax
import jax.numpy as jnp
import numpy as np
from jax import lax
from jax.experimental import pallas as pl
from jax.experimental.pallas import tpu as pltpu
from jax.sharding import PartitionSpec as P

MX = 32
MY = 32
MZ = 32


KAPPA = 0.7978845608028654
CUBIC = 0.044715


def gelu_slope(value):
    inner = KAPPA * (value + CUBIC * value * value * value)
    tangent = jnp.tanh(inner)
    result = 0.5 * value * (1.0 + tangent)
    slope = 0.5 * (1.0 + tangent) + 0.5 * value * (1.0 - tangent * tangent) * KAPPA * (
        1.0 + 3.0 * CUBIC * value * value
    )
    return (result, slope)


def trig_pair(freqs, length):
    positions = jnp.arange(length, dtype=jnp.int32)
    turns = positions[:, None] * (freqs[None, :] % length) % length
    angle = turns.astype(jnp.float32) * (2.0 * math.pi / length)
    factor = 1.0 / math.sqrt(length)
    return (jnp.cos(angle) * factor, jnp.sin(angle) * factor)


def real_table(freqs, length):
    cosine, sine = trig_pair(freqs, length)
    return jnp.stack([cosine.T, -sine.T]).astype(jnp.bfloat16)


def complex_table(freqs, length):
    cosine, sine = trig_pair(freqs, length)
    upper = jnp.stack([cosine, -sine], axis=1)
    lower = jnp.stack([sine, cosine], axis=1)
    return jnp.stack([upper, lower]).astype(jnp.bfloat16)


def centered(count):
    return jnp.arange(count, dtype=jnp.int32) - count // 2


def to_modes(values, tables):
    z_table, y_table, x_table = tables
    chans, xrows, yrows, zlen = values.shape
    first = jnp.einsum("cxyn,qkn->qkycx", values, z_table, preferred_element_type=jnp.float32)
    first = first.astype(jnp.bfloat16).reshape(2, MZ, yrows, chans * xrows)
    moved = lax.all_to_all(first, ("gy", "col"), split_axis=1, concat_axis=2, tiled=True)
    second = jnp.einsum("pkyr,pyqj->qkjr", moved, y_table, preferred_element_type=jnp.float32)
    second = second.astype(jnp.bfloat16)[:, :, :, None, :]
    crossed = lax.all_to_all(second, "gx", split_axis=2, concat_axis=3, tiled=True)
    crossed = crossed.reshape(crossed.shape[:4] + (chans, xrows))
    third = jnp.einsum("pkjgcx,pgxql->qckjl", crossed, x_table, preferred_element_type=jnp.float32)
    return third.astype(jnp.bfloat16).reshape(2, chans, -1)


def to_grid(spec, tables, shape, local_modes):
    z_table, y_table, x_table = tables
    chans, xrows, yrows, zlen = shape
    spec = spec.reshape((2, chans) + local_modes)
    first = jnp.einsum("pckjl,qgxpl->qkjgcx", spec, x_table, preferred_element_type=jnp.float32)
    first = first.astype(jnp.bfloat16)
    first = first.reshape(first.shape[:4] + (chans * xrows,))
    joined = lax.all_to_all(first, "gx", split_axis=3, concat_axis=2, tiled=True)
    joined = joined.reshape(joined.shape[:3] + (chans * xrows,))
    second = jnp.einsum("pkjr,qypj->qkyr", joined, y_table, preferred_element_type=jnp.float32)
    second = second.astype(jnp.bfloat16)
    returned = lax.all_to_all(second, ("gy", "col"), split_axis=2, concat_axis=1, tiled=True)
    grid = jnp.einsum("pkyr,pkn->ryn", returned, z_table, preferred_element_type=jnp.float32)
    return grid.reshape(chans, xrows, yrows, zlen)


def mix(weight, modes):
    real = jnp.einsum("iok,ik->ok", weight[0], modes[0], preferred_element_type=jnp.float32)
    real = real - jnp.einsum("iok,ik->ok", weight[1], modes[1], preferred_element_type=jnp.float32)
    imag = jnp.einsum("iok,ik->ok", weight[0], modes[1], preferred_element_type=jnp.float32)
    imag = imag + jnp.einsum("iok,ik->ok", weight[1], modes[0], preferred_element_type=jnp.float32)
    return jnp.stack([real, imag]).astype(jnp.bfloat16)


def on_device_plain(field, cotangent, mode_weight, skip_weight, lift_weight, proj_weight):
    chans, xrows, yrows, zlen = field.shape
    groups_x = lax.axis_size("gx")
    groups_y = lax.axis_size("gy")
    groups_c = lax.axis_size("col")
    span_x = xrows * groups_x
    span_y = yrows * groups_y * groups_c
    column = jnp.arange(MZ, dtype=jnp.int32)
    z_table = real_table(column, zlen)
    y_table = complex_table(centered(MY), span_y)
    x_table = complex_table(centered(MX), span_x).reshape(2, groups_x, xrows, 2, MX)
    tables = (z_table, y_table, x_table)
    local_modes = (mode_weight.shape[3], mode_weight.shape[4], mode_weight.shape[5])
    weight_flat = mode_weight.reshape(2, chans, chans, -1)
    modes = to_modes(field, tables)
    spectral = to_grid(mix(weight_flat, modes), tables, field.shape, local_modes).reshape(chans, -1)
    flat_field = field.reshape(chans, -1)
    flat_grad = cotangent.reshape(chans, -1)
    pre = spectral + jnp.dot(skip_weight, flat_field, preferred_element_type=jnp.float32)
    lifted, slope_pre = gelu_slope(pre)
    lifted = lifted.astype(jnp.bfloat16)
    hidden = jnp.dot(lift_weight, lifted, preferred_element_type=jnp.float32)
    activated, slope_hid = gelu_slope(hidden)
    activated = activated.astype(jnp.bfloat16)
    back_hidden = jnp.dot(proj_weight.T, flat_grad, preferred_element_type=jnp.float32)
    hidden_grad = (back_hidden * slope_hid).astype(jnp.bfloat16)
    grad_up = flat_grad.astype(jnp.float32) + jnp.dot(
        lift_weight.T, hidden_grad, preferred_element_type=jnp.float32
    )
    pre_grad = (grad_up * slope_pre).astype(jnp.bfloat16)
    proj_part = jnp.einsum("cr,hr->ch", flat_grad, activated, preferred_element_type=jnp.float32)
    lift_part = jnp.einsum("hr,cr->hc", hidden_grad, lifted, preferred_element_type=jnp.float32)
    skip_part = jnp.einsum("or,ir->oi", pre_grad, flat_field, preferred_element_type=jnp.float32)
    proj_grad, lift_grad, skip_grad = lax.psum(
        (proj_part, lift_part, skip_part), ("gx", "gy", "col")
    )
    pre_modes = to_modes(pre_grad.reshape(field.shape), tables)
    grad_real = jnp.einsum("ik,ok->iok", modes[0], pre_modes[0], preferred_element_type=jnp.float32)
    grad_real = grad_real + jnp.einsum(
        "ik,ok->iok", modes[1], pre_modes[1], preferred_element_type=jnp.float32
    )
    grad_imag = jnp.einsum("ik,ok->iok", modes[0], pre_modes[1], preferred_element_type=jnp.float32)
    grad_imag = grad_imag - jnp.einsum(
        "ik,ok->iok", modes[1], pre_modes[0], preferred_element_type=jnp.float32
    )
    mode_grad = jnp.stack([grad_real, grad_imag]).astype(jnp.bfloat16).reshape(mode_weight.shape)
    back_real = jnp.einsum(
        "iok,ok->ik", weight_flat[0], pre_modes[0], preferred_element_type=jnp.float32
    )
    back_real = back_real + jnp.einsum(
        "iok,ok->ik", weight_flat[1], pre_modes[1], preferred_element_type=jnp.float32
    )
    back_imag = jnp.einsum(
        "iok,ok->ik", weight_flat[0], pre_modes[1], preferred_element_type=jnp.float32
    )
    back_imag = back_imag - jnp.einsum(
        "iok,ok->ik", weight_flat[1], pre_modes[0], preferred_element_type=jnp.float32
    )
    modes_grad = jnp.stack([back_real, back_imag]).astype(jnp.bfloat16)
    spectral_grad = to_grid(modes_grad, tables, field.shape, local_modes).reshape(chans, -1)
    skip_back = jnp.dot(skip_weight.T, pre_grad, preferred_element_type=jnp.float32)
    field_grad = (spectral_grad + skip_back).astype(jnp.bfloat16).reshape(field.shape)
    return (field_grad, mode_grad, skip_grad, lift_grad, proj_grad)


F32 = jnp.float32
BF16 = jnp.bfloat16
LANES = 128


def np_trig(freqs, length):
    turns = (np.arange(length)[:, None] * (freqs[None, :] % length)) % length
    angle = turns.astype(np.float32) * np.float32(2.0 * math.pi / length)
    factor = np.float32(1.0 / math.sqrt(length))
    return (np.cos(angle) * factor, np.sin(angle) * factor)


def np_complex(freqs, length):
    cosine, sine = np_trig(freqs, length)
    upper = np.stack([cosine, -sine], axis=1)
    lower = np.stack([sine, cosine], axis=1)
    return np.stack([upper, lower])


def host_tables(zlen, yrows, xrows, n_z, n_y, half):
    cosine, sine = np_trig(np.arange(MZ), zlen)
    z_pair = np.stack([cosine.T, -sine.T], axis=1).reshape(2 * MZ, zlen)
    y_full = np_complex(np.arange(MY) - MY // 2, yrows * n_z)
    kyb = MY // n_y
    y_six = y_full.reshape(2, n_z, yrows, 2, n_y, kyb)
    y_fwd = y_six.transpose(4, 3, 5, 1, 0, 2).reshape(2 * MY, 2 * yrows * n_z)
    y_inv = y_six.transpose(1, 0, 2, 4, 3, 5).reshape(2 * yrows * n_z, 2 * MY)
    x_full = np_complex(np.arange(MX) - MX // 2, xrows * n_y).reshape(2, n_y, xrows, 2, MX)
    x_rows = x_full.transpose(1, 0, 2, 3, 4).reshape(n_y, 2, xrows, 1, 2 * MX)
    x_rows = np.broadcast_to(x_rows, (n_y, 2, xrows, half, 2 * MX)).reshape(-1, 2 * MX)
    x_fwd = np.concatenate([x_rows, x_rows], axis=1)
    x_cols = x_full.transpose(3, 4, 1, 0, 2).reshape(2 * MX, n_y, 2, xrows, 1)
    x_inv = np.broadcast_to(x_cols, (2 * MX, n_y, 2, xrows, half)).reshape(2 * MX, -1)
    return [
        jnp.asarray(np.ascontiguousarray(table), BF16)
        for table in (z_pair, y_fwd, y_inv, x_fwd, x_inv)
    ]


def dot(left, right, dims=((1,), (0,))):
    return lax.dot_general(left, right, (dims, ((), ())), preferred_element_type=F32)


NT = ((1,), (1,))
TN = ((0,), (0,))


def gelu_pair(value):
    square = value * value
    tangent = jnp.tanh(value * (KAPPA + (KAPPA * CUBIC) * square))
    half = 0.5 + 0.5 * tangent
    result = value * half
    slope = half + result * (1.0 - tangent) * (KAPPA + (3.0 * KAPPA * CUBIC) * square)
    return (result, slope)


def layer_kernel(
    geo, field_ref, cot_ref, weight_ref, skip_ref, lift_ref, proj_ref,
    tz_ref, tyf_ref, tyi_ref, txf_ref, txi_ref,
    grad_ref, modes_out, premodes_out, sums_out,
    held, packed, dense, cells, cots, cot_in, pgrad, kxf, kxi, spec_grid, mixed, spread,
    modes_ref, premodes_ref, send_z, recv_z, send_y, recv_y, sums, sums_x, sums_z,
    weight_sem, own_sem, send_sem, recv_sem, io_sem,
):
    n_gy, n_col, n_y, chans, xrows, yrows, kzb, kyb = geo
    n_z = n_gy * n_col
    half = LANES // xrows
    parts = chans // half
    zlen = cells.shape[-1]
    my_gy, my_col, my_gx = lax.axis_index("gy"), lax.axis_index("col"), lax.axis_index("gx")
    me_z, me_y = my_gy * n_col + my_col, my_gx

    folds = LANES // MX
    fold_rows = kzb * kyb // folds
    loads = weight_sem.shape[0]
    load_chans = chans // loads

    def weight_load(index):
        span = pl.ds(index * load_chans, load_chans)
        return pltpu.make_async_copy(
            weight_ref.at[:, span], held.at[:, span], weight_sem.at[index]
        )

    cot_load = pltpu.make_async_copy(cot_ref, cot_in, io_sem.at[0])
    cot_load.start()
    for index in range(loads):
        weight_load(index).start()

    def fold(tall):
        return jnp.concatenate(
            [tall[at * fold_rows:(at + 1) * fold_rows] for at in range(folds)], axis=1
        )

    block_of = lax.broadcasted_iota(jnp.int32, (fold_rows, LANES), 1) // MX

    def shifts(tiles):
        return [
            [tile] + [pltpu.roll(tile, step * MX, 1) for step in range(1, folds)] for tile in tiles
        ]

    def swap_blocks(moved):
        swapped = []
        for lane in range(folds):
            total = moved[0][-lane % folds]
            for row in range(1, folds):
                total = jnp.where(block_of == row, moved[row][(row - lane) % folds], total)
            swapped.append(total)
        return swapped

    def pack_weight(index):
        weight_load(index).wait()
        outs = 8

        def body(block, carry):
            first = block * outs
            for chan in range(index * load_chans, (index + 1) * load_chans):
                for piece in range(2):
                    for out in range(outs):
                        packed[piece, chan, first + out] = fold(held[piece, chan, first + out])
            return carry

        lax.fori_loop(0, chans // outs, body, 0)

    def peer_z(step):
        other = lax.rem(me_z + step, n_z)
        return other, {"gy": other // n_col, "col": lax.rem(other, n_col)}

    def peer_y(step):
        other = lax.rem(me_y + step, n_y)
        return other, {"gx": other}

    barrier = pltpu.get_barrier_semaphore()
    for step in range(1, n_z):
        pl.semaphore_signal(
            barrier, inc=1, device_id=peer_z(step)[1], device_id_type=pl.DeviceIdType.MESH
        )
    for step in range(1, n_y):
        pl.semaphore_signal(
            barrier, inc=1, device_id=peer_y(step)[1], device_id_type=pl.DeviceIdType.MESH
        )

    def exchange(slot, send, recv, count, me, peer):
        copies = []
        for step in range(1, count):
            other, where = peer(step)
            copy = pltpu.make_async_remote_copy(
                src_ref=send.at[other],
                dst_ref=recv.at[me],
                send_sem=send_sem.at[slot, step],
                recv_sem=recv_sem.at[slot, step],
                device_id=where,
                device_id_type=pl.DeviceIdType.MESH,
            )
            copy.start()
            copies.append(copy)
        own = pltpu.make_async_copy(send.at[me], recv.at[me], own_sem.at[slot])
        own.start()
        copies.append(own)
        return copies

    def exchange_z(phase, part):
        return exchange(
            2 * phase * parts + part, send_z.at[phase, part], recv_z.at[phase, part],
            n_z, me_z, peer_z,
        )

    def exchange_y(phase, part):
        return exchange(
            (2 * phase + 1) * parts + part, send_y.at[phase, part], recv_y.at[phase, part],
            n_y, me_y, peer_y,
        )

    def finish(copies):
        for copy in copies:
            copy.wait()

    def cells_first(source, target):
        for cell in range(xrows):
            rows = source[:, cell, :, :].astype(F32)
            target[:, cell] = jnp.transpose(rows, (1, 0, 2)).astype(BF16)

    def chans_of(part):
        return slice(part * half, (part + 1) * half)

    def start_z(source, phase, part):
        planes = [
            dot(tz_ref[...], source[row, :, chans_of(part), :].reshape(LANES, zlen), NT)
            for row in range(yrows)
        ]
        turned = jnp.transpose(jnp.stack(planes), (1, 0, 2))
        turned = turned.reshape(n_z, kzb, 2 * yrows, LANES).astype(BF16)
        for block in range(n_z):
            send_z[phase, part, block] = jnp.concatenate(
                [turned[block, freq] for freq in range(kzb)], axis=1
            )
        return exchange_z(phase, part)

    def start_y(phase, part):
        rows = recv_z[phase, part].reshape(n_z * 2 * yrows, kzb * LANES)
        moved = dot(tyf_ref[...], rows).astype(BF16)
        send_y[phase, part] = moved.reshape(n_y, 2 * kyb, kzb * LANES)
        return exchange_y(phase, part)

    def reach_modes(phase, part, target):
        blocks = [recv_y[phase, part, group].astype(F32) for group in range(n_y)]
        columns = []
        for group in range(n_y):
            for piece in range(2):
                tiles = [
                    blocks[group][
                        piece * kyb:(piece + 1) * kyb, freq * LANES:(freq + 1) * LANES
                    ]
                    for freq in range(kzb)
                ]
                columns.append(jnp.concatenate(tiles, axis=0).astype(BF16))
        result = dot(jnp.concatenate(columns, axis=1), kxf[...])
        for tile in range(half * 2 * MX // LANES):
            tiles = [
                result[row * fold_rows:(row + 1) * fold_rows, tile * LANES:(tile + 1) * LANES]
                for row in range(folds)
            ]
            moved = shifts(tiles)
            swapped = swap_blocks(moved)
            for lane in range(folds):
                chan, piece = divmod(tile * folds + lane, 2)
                dense[piece, part * half + chan] = swapped[lane].astype(BF16)
                for row in range(folds):
                    target[
                        piece, part * half + chan, row * fold_rows:(row + 1) * fold_rows, :
                    ] = moved[row][-lane % folds][:, :MX].astype(BF16)

    run = 4

    def mix(summed_part, out_part):
        def body(index, carry):
            at = summed_part * half + index * run
            real = [dense[0, at + step] for step in range(run)]
            imag = [dense[1, at + step] for step in range(run)]
            for out in range(out_part * half, (out_part + 1) * half):
                short = [None, None]
                for step in range(run):
                    w_real, w_imag = packed[0, at + step, out], packed[1, at + step, out]
                    new = (
                        w_real * real[step] - w_imag * imag[step],
                        w_real * imag[step] + w_imag * real[step],
                    )
                    for piece in range(2):
                        old = short[piece]
                        short[piece] = new[piece] if old is None else old + new[piece]
                for piece in range(2):
                    mixed[piece, out] += short[piece].astype(F32)
            return carry

        lax.fori_loop(0, half // run, body, 0)

    def mix_back(summed_part, out_part):
        outs = 4

        def body(index, carry):
            first = out_part * half + index * outs
            total = [[mixed[piece, first + out] for piece in range(2)] for out in range(outs)]
            short = [[None, None] for _ in range(outs)]
            for step in range(half):
                summed = summed_part * half + step
                real, imag = dense[0, summed], dense[1, summed]
                for out in range(outs):
                    w_real, w_imag = packed[0, first + out, summed], packed[1, first + out, summed]
                    new = (w_real * real + w_imag * imag, w_real * imag - w_imag * real)
                    for piece in range(2):
                        old = short[out][piece]
                        short[out][piece] = new[piece] if old is None else old + new[piece]
                        if (step + 1) % run == 0:
                            total[out][piece] = total[out][piece] + short[out][piece].astype(F32)
                            short[out][piece] = None
            for out in range(outs):
                for piece in range(2):
                    mixed[piece, first + out] = total[out][piece]
            return carry

        lax.fori_loop(0, half // outs, body, 0)

    def start_back_x(phase, part):
        for tile in range(half * 2 * MX // LANES):
            tiles = []
            for lane in range(folds):
                chan, piece = divmod(tile * folds + lane, 2)
                tiles.append(mixed[piece, part * half + chan])
            swapped = swap_blocks(shifts(tiles))
            for row in range(folds):
                spread[
                    part, row * fold_rows:(row + 1) * fold_rows, tile * LANES:(tile + 1) * LANES
                ] = swapped[row].astype(BF16)
        both = dot(spread[part], kxi[...])
        for group in range(n_y):
            rows = []
            for piece in range(2):
                at = (group * 2 + piece) * LANES
                rows.append(jnp.concatenate(
                    [both[freq * kyb:(freq + 1) * kyb, at:at + LANES] for freq in range(kzb)],
                    axis=1,
                ))
            send_y[phase, part, group] = jnp.concatenate(rows, axis=0).astype(BF16)
        return exchange_y(phase, part)

    def start_back_y(phase, part):
        rows = recv_y[phase, part].reshape(n_y * 2 * kyb, kzb * LANES)
        moved = dot(tyi_ref[...], rows).astype(BF16)
        send_z[phase, part] = moved.reshape(n_z, 2 * yrows, kzb * LANES)
        return exchange_z(phase, part)

    def reach_grid(phase, part, emit):
        tiles = []
        for block in range(n_z):
            rows = recv_z[phase, part, block].astype(F32)
            for freq in range(kzb):
                for piece in range(2):
                    tiles.append(
                        rows[piece * yrows:(piece + 1) * yrows, freq * LANES:(freq + 1) * LANES]
                    )
        turned = jnp.transpose(jnp.stack(tiles), (1, 0, 2)).astype(BF16)
        for row in range(yrows):
            emit(row, part, dot(turned[row], tz_ref[...], TN).reshape(xrows, half, zlen))

    def keep_grid(row, part, values):
        spec_grid[row, :, chans_of(part), :] = values

    def keep_grad(row, part, values):
        total = values + spec_grid[row, :, chans_of(part), :]
        grad_ref[row, :, chans_of(part), :] = total.astype(BF16)

    def wide_cells(ref, row):
        return jnp.concatenate([ref[row, cell] for cell in range(xrows)], axis=1)

    def build_x_tables():
        tall, wide = kxf.shape
        lane = lax.broadcasted_iota(jnp.int32, (tall, LANES), 1)
        line = lax.broadcasted_iota(jnp.int32, (tall, LANES), 0)
        owner = line % half
        pair = txf_ref[...].astype(F32)
        per_tile = LANES // (2 * MX)
        for tile in range(wide // LANES):
            keep = owner == tile * per_tile + lane // (2 * MX)
            kxf[:, tile * LANES:(tile + 1) * LANES] = jnp.where(keep, pair, 0.0).astype(BF16)
        flat = txi_ref[...].astype(F32)
        lane_owner = lax.broadcasted_iota(jnp.int32, flat.shape, 1) % half
        for chan in range(half):
            kxi[chan * 2 * MX:(chan + 1) * 2 * MX, :] = jnp.where(
                lane_owner == chan, flat, 0.0
            ).astype(BF16)

    both = range(parts)
    clear = jnp.zeros(mixed.shape, F32)
    cells_first(field_ref, cells)
    pl.semaphore_wait(barrier, n_z - 1 + n_y - 1)
    going_z = [start_z(cells, 0, part) for part in both]
    build_x_tables()
    mixed[...] = clear
    cot_load.wait()
    cells_first(cot_in, cots)
    early = loads // 4
    for index in range(early):
        pack_weight(index)
    going_y = []
    for part in both:
        finish(going_z[part])
        going_y.append(start_y(0, part))
    for index in range(early, loads):
        pack_weight(index)
    for part in both:
        finish(going_y[part])
        reach_modes(0, part, modes_ref)
        if part < parts - 1:
            for out_part in both:
                mix(part, out_part)
    modes_save = pltpu.make_async_copy(modes_ref, modes_out, io_sem.at[1])
    modes_save.start()
    going_y = []
    for part in both:
        mix(parts - 1, part)
        going_y.append(start_back_x(1, part))
    going_z = []
    for part in both:
        finish(going_y[part])
        going_z.append(start_back_y(1, part))
    sums[...] = jnp.zeros(sums.shape, F32)
    mixed[...] = clear
    for part in both:
        finish(going_z[part])
        reach_grid(1, part, keep_grid)

    pair = 2

    def pointwise(step, carry):
        lines = [step * pair + line for line in range(pair)]
        values = jnp.concatenate([wide_cells(cells, row) for row in lines], axis=1)
        grads = jnp.concatenate([wide_cells(cots, row) for row in lines], axis=1)
        spec = jnp.concatenate(
            [spec_grid[row, cell] for row in lines for cell in range(xrows)], axis=1
        )
        pre = spec + dot(skip_ref[...], values)
        lifted, slope_pre = gelu_pair(pre)
        lifted = lifted.astype(BF16)
        hidden = dot(lift_ref[...], lifted, TN)
        activated, slope_hid = gelu_pair(hidden)
        activated = activated.astype(BF16)
        hidden_grad = (dot(proj_ref[...], grads, TN) * slope_hid).astype(BF16)
        grad_up = grads.astype(F32) + dot(lift_ref[...], hidden_grad)
        pre_grad = (grad_up * slope_pre).astype(BF16)
        sums[0:chans] += dot(grads, activated, NT)
        sums[chans:2 * chans] += dot(lifted, hidden_grad, NT)
        sums[2 * chans:, 0:chans] += dot(pre_grad, values, NT)
        for line in range(pair):
            for cell in range(xrows):
                at = (line * xrows + cell) * zlen
                pgrad[lines[line], cell] = pre_grad[:, at:at + zlen]
        return carry

    lax.fori_loop(0, yrows // pair, pointwise, 0)

    share = sums.shape[0] // n_y
    spare = 8 * parts

    def send_sums(slot, count, me, peer, source, target):
        copies = []
        for step in range(1, count):
            other, where = peer(step)
            copy = pltpu.make_async_remote_copy(
                src_ref=source(other),
                dst_ref=target.at[me],
                send_sem=send_sem.at[slot, step],
                recv_sem=recv_sem.at[slot, step],
                device_id=where,
                device_id_type=pl.DeviceIdType.MESH,
            )
            copy.start()
            copies.append(copy)
        return copies

    def rows_of(index):
        return pl.ds(pl.multiple_of(index * share, 8), share)

    def skip_back(row, carry):
        total = dot(skip_ref[...], wide_cells(pgrad, row), TN)
        for cell in range(xrows):
            spec_grid[row, cell] = total[:, cell * zlen:(cell + 1) * zlen]
        return carry

    going_z = [start_z(pgrad, 2, part) for part in both]
    sums_x[me_y] = sums[rows_of(me_y), :]
    small = send_sums(spare, n_y, me_y, peer_y, lambda other: sums.at[rows_of(other)], sums_x)
    going_y = []
    for part in both:
        finish(going_z[part])
        going_y.append(start_y(2, part))
    finish(small)
    sums_z[me_z] = jnp.sum(sums_x[...], axis=0)
    small = send_sums(spare + 1, n_z, me_z, peer_z, lambda other: sums_z.at[me_z], sums_z)
    lax.fori_loop(0, yrows, skip_back, 0)
    for part in both:
        finish(going_y[part])
        reach_modes(2, part, premodes_ref)
        if part < parts - 1:
            for out_part in both:
                mix_back(part, out_part)
    premodes_save = pltpu.make_async_copy(premodes_ref, premodes_out, io_sem.at[2])
    premodes_save.start()
    going_y = []
    for part in both:
        mix_back(parts - 1, part)
        going_y.append(start_back_x(3, part))
    finish(small)
    sums_out[me_y] = jnp.sum(sums_z[...], axis=0)
    small = send_sums(spare + 2, n_y, me_y, peer_y, lambda other: sums_out.at[me_y], sums_out)
    going_z = []
    for part in both:
        finish(going_y[part])
        going_z.append(start_back_y(3, part))
    finish(small)
    modes_save.wait()
    premodes_save.wait()
    for part in both:
        finish(going_z[part])
        reach_grid(3, part, keep_grad)


def outer_kernel(
    modes_ref, pre_ref, grid_ref, sums_ref, out_ref, field_ref, proj_ref, lift_ref, skip_ref
):
    chans, rows = pre_ref.shape[1], pre_ref.shape[2]

    def body(out, carry):
        for top in range(0, rows, 16):
            p_real, p_imag = pre_ref[0, out, top:top + 16], pre_ref[1, out, top:top + 16]
            for chan in range(modes_ref.shape[1]):
                m_real, m_imag = modes_ref[0, chan, top:top + 16], modes_ref[1, chan, top:top + 16]
                out_ref[0, chan, out, top:top + 16] = m_real * p_real + m_imag * p_imag
                out_ref[1, chan, out, top:top + 16] = m_real * p_imag - m_imag * p_real
        return carry

    lax.fori_loop(0, chans, body, 0)
    for cell in range(grid_ref.shape[1]):
        cells = grid_ref[:, cell].astype(F32)
        field_ref[:, cell] = jnp.transpose(cells, (1, 0, 2)).astype(BF16)
    proj_ref[...] = sums_ref[0:chans]
    lift_ref[...] = sums_ref[chans:2 * chans]
    skip_ref[...] = sums_ref[2 * chans:, 0:chans]


def finish_gradients(modes, pre_modes, grid, sums):
    _, chans, rows, lanes = modes.shape
    yrows, xrows, _, zlen = grid.shape
    steps = math.gcd(chans, xrows)
    group, cells = chans // steps, xrows // steps
    return pl.pallas_call(
        outer_kernel,
        grid=(steps,),
        in_specs=[
            pl.BlockSpec((2, group, rows, lanes), lambda step: (0, step, 0, 0)),
            pl.BlockSpec((2, chans, rows, lanes), lambda step: (0, 0, 0, 0)),
            pl.BlockSpec((yrows, cells, chans, zlen), lambda step: (0, step, 0, 0)),
            pl.BlockSpec(sums.shape, lambda step: (0, 0)),
        ],
        out_specs=[
            pl.BlockSpec((2, group, chans, rows, lanes), lambda step: (0, step, 0, 0, 0)),
            pl.BlockSpec((chans, cells, yrows, zlen), lambda step: (0, step, 0, 0)),
            pl.BlockSpec((chans, LANES), lambda step: (0, 0)),
            pl.BlockSpec((chans, LANES), lambda step: (0, 0)),
            pl.BlockSpec((chans, chans), lambda step: (0, 0)),
        ],
        out_shape=(
            jax.ShapeDtypeStruct((2, chans, chans, rows, lanes), BF16),
            jax.ShapeDtypeStruct((chans, xrows, yrows, zlen), BF16),
            jax.ShapeDtypeStruct((chans, LANES), F32),
            jax.ShapeDtypeStruct((chans, LANES), F32),
            jax.ShapeDtypeStruct((chans, chans), F32),
        ),
        compiler_params=pltpu.CompilerParams(vmem_limit_bytes=60 << 20),
        name="mode_outer",
    )(modes, pre_modes, grid, sums)


def on_device(field, cotangent, mode_weight, skip_weight, lift_weight, proj_weight):
    chans, xrows, yrows, zlen = field.shape
    kzb, kyb = mode_weight.shape[3], mode_weight.shape[4]
    n_gy, n_col, n_y = lax.axis_size("gy"), lax.axis_size("col"), lax.axis_size("gx")
    n_z = n_gy * n_col
    fits = kyb == 8 and kzb % 2 == 0 and xrows == 8 and yrows == 8 and zlen == LANES
    fits = fits and lift_weight.shape[0] == LANES and (3 * chans) % (8 * n_y) == 0 and chans % 8 == 0
    fits = fits and (kzb * kyb * MX) % (16 * LANES) == 0
    if not fits or 2 * MX * 2 != LANES or chans % (LANES // xrows) or LANES // xrows != 16:
        return on_device_plain(
            field, cotangent, mode_weight, skip_weight, lift_weight, proj_weight
        )
    half = LANES // xrows
    parts = chans // half
    rows = kzb * kyb
    tables = host_tables(zlen, yrows, xrows, n_z, n_y, half)
    weight = mode_weight.reshape(2, chans, chans, rows, MX)
    share = 3 * chans // n_y
    vmem = pl.BlockSpec(memory_space=pltpu.VMEM)
    hbm = pl.BlockSpec(memory_space=pl.ANY)
    geo = (n_gy, n_col, n_y, chans, xrows, yrows, kzb, kyb)
    grid_shape = (yrows, xrows, chans, zlen)
    spectral = (2, chans, rows, MX)
    packed = (2, chans, rows * MX // LANES, LANES)
    outs = pl.pallas_call(
        functools.partial(layer_kernel, geo),
        out_shape=(
            jax.ShapeDtypeStruct(grid_shape, BF16),
            jax.ShapeDtypeStruct(spectral, BF16),
            jax.ShapeDtypeStruct(spectral, BF16),
            jax.ShapeDtypeStruct((n_y, share, LANES), F32),
        ),
        in_specs=[vmem, hbm, hbm] + [vmem] * 8,
        out_specs=(vmem, hbm, hbm, vmem),
        scratch_shapes=[
            pltpu.VMEM(weight.shape, BF16),
            pltpu.VMEM((2, chans, chans, rows * MX // LANES, LANES), BF16),
            pltpu.VMEM(packed, BF16),
            pltpu.VMEM(grid_shape, BF16),
            pltpu.VMEM(grid_shape, BF16),
            pltpu.VMEM(cotangent.shape, BF16),
            pltpu.VMEM(grid_shape, BF16),
            pltpu.VMEM((n_y * 2 * LANES, half * 2 * MX), BF16),
            pltpu.VMEM((half * 2 * MX, n_y * 2 * LANES), BF16),
            pltpu.VMEM(grid_shape, F32),
            pltpu.VMEM(packed, F32),
            pltpu.VMEM((parts, rows, half * 2 * MX), BF16),
            pltpu.VMEM(spectral, BF16),
            pltpu.VMEM(spectral, BF16),
            pltpu.VMEM((4, parts, n_z, 2 * yrows, kzb * LANES), BF16),
            pltpu.VMEM((4, parts, n_z, 2 * yrows, kzb * LANES), BF16),
            pltpu.VMEM((4, parts, n_y, 2 * kyb, kzb * LANES), BF16),
            pltpu.VMEM((4, parts, n_y, 2 * kyb, kzb * LANES), BF16),
            pltpu.VMEM((n_y * share, LANES), F32),
            pltpu.VMEM((n_y, share, LANES), F32),
            pltpu.VMEM((n_z, share, LANES), F32),
            pltpu.SemaphoreType.DMA((8,)),
            pltpu.SemaphoreType.DMA((8 * parts,)),
            pltpu.SemaphoreType.DMA((8 * parts + 3, max(n_z, n_y))),
            pltpu.SemaphoreType.DMA((8 * parts + 3, max(n_z, n_y))),
            pltpu.SemaphoreType.DMA((3,)),
        ],
        compiler_params=pltpu.CompilerParams(
            collective_id=0, has_side_effects=True, vmem_limit_bytes=62 << 20
        ),
        name="spectral_layer",
    )(field, cotangent, weight, skip_weight, lift_weight.T, proj_weight, *tables)
    grad, modes, pre_modes, sums = outs
    mode_grad, field_grad, proj_grad, lift_turned, skip_grad = finish_gradients(
        modes, pre_modes, grad, sums.reshape(3 * chans, LANES)
    )
    return (field_grad, mode_grad.reshape(mode_weight.shape), skip_grad, lift_turned.T, proj_grad)


def solution(mesh):
    in_specs = (
        P("grp", "gx", ("gy", "col"), None),
        P("grp", "gx", ("gy", "col"), None),
        P(None, None, None, ("gy", "col"), "gx", None),
        P(),
        P(),
        P(),
    )
    out_specs = (
        P("grp", "gx", ("gy", "col"), None),
        P("grp", None, None, ("gy", "col"), "gx", None),
        P("grp", None),
        P("grp", None),
        P("grp", None),
    )
    return jax.shard_map(
        on_device, mesh=mesh, in_specs=in_specs, out_specs=out_specs, check_vma=False
    )
```

```python
import functools
import math

import jax
import jax.numpy as jnp
import numpy as np
from jax import lax
from jax.experimental import pallas as pl
from jax.experimental.pallas import tpu as pltpu
from jax.sharding import PartitionSpec as P

MX = 32
MY = 32
MZ = 32


KAPPA = 0.7978845608028654
CUBIC = 0.044715


def gelu_slope(value):
    inner = KAPPA * (value + CUBIC * value * value * value)
    tangent = jnp.tanh(inner)
    result = 0.5 * value * (1.0 + tangent)
    slope = 0.5 * (1.0 + tangent) + 0.5 * value * (1.0 - tangent * tangent) * KAPPA * (
        1.0 + 3.0 * CUBIC * value * value
    )
    return (result, slope)


def trig_pair(freqs, length):
    positions = jnp.arange(length, dtype=jnp.int32)
    turns = positions[:, None] * (freqs[None, :] % length) % length
    angle = turns.astype(jnp.float32) * (2.0 * math.pi / length)
    factor = 1.0 / math.sqrt(length)
    return (jnp.cos(angle) * factor, jnp.sin(angle) * factor)


def real_table(freqs, length):
    cosine, sine = trig_pair(freqs, length)
    return jnp.stack([cosine.T, -sine.T]).astype(jnp.bfloat16)


def complex_table(freqs, length):
    cosine, sine = trig_pair(freqs, length)
    upper = jnp.stack([cosine, -sine], axis=1)
    lower = jnp.stack([sine, cosine], axis=1)
    return jnp.stack([upper, lower]).astype(jnp.bfloat16)


def centered(count):
    return jnp.arange(count, dtype=jnp.int32) - count // 2


def to_modes(values, tables):
    z_table, y_table, x_table = tables
    chans, xrows, yrows, zlen = values.shape
    first = jnp.einsum("cxyn,qkn->qkycx", values, z_table, preferred_element_type=jnp.float32)
    first = first.astype(jnp.bfloat16).reshape(2, MZ, yrows, chans * xrows)
    moved = lax.all_to_all(first, ("gy", "col"), split_axis=1, concat_axis=2, tiled=True)
    second = jnp.einsum("pkyr,pyqj->qkjr", moved, y_table, preferred_element_type=jnp.float32)
    second = second.astype(jnp.bfloat16)[:, :, :, None, :]
    crossed = lax.all_to_all(second, "gx", split_axis=2, concat_axis=3, tiled=True)
    crossed = crossed.reshape(crossed.shape[:4] + (chans, xrows))
    third = jnp.einsum("pkjgcx,pgxql->qckjl", crossed, x_table, preferred_element_type=jnp.float32)
    return third.astype(jnp.bfloat16).reshape(2, chans, -1)


def to_grid(spec, tables, shape, local_modes):
    z_table, y_table, x_table = tables
    chans, xrows, yrows, zlen = shape
    spec = spec.reshape((2, chans) + local_modes)
    first = jnp.einsum("pckjl,qgxpl->qkjgcx", spec, x_table, preferred_element_type=jnp.float32)
    first = first.astype(jnp.bfloat16)
    first = first.reshape(first.shape[:4] + (chans * xrows,))
    joined = lax.all_to_all(first, "gx", split_axis=3, concat_axis=2, tiled=True)
    joined = joined.reshape(joined.shape[:3] + (chans * xrows,))
    second = jnp.einsum("pkjr,qypj->qkyr", joined, y_table, preferred_element_type=jnp.float32)
    second = second.astype(jnp.bfloat16)
    returned = lax.all_to_all(second, ("gy", "col"), split_axis=2, concat_axis=1, tiled=True)
    grid = jnp.einsum("pkyr,pkn->ryn", returned, z_table, preferred_element_type=jnp.float32)
    return grid.reshape(chans, xrows, yrows, zlen)


def mix(weight, modes):
    real = jnp.einsum("iok,ik->ok", weight[0], modes[0], preferred_element_type=jnp.float32)
    real = real - jnp.einsum("iok,ik->ok", weight[1], modes[1], preferred_element_type=jnp.float32)
    imag = jnp.einsum("iok,ik->ok", weight[0], modes[1], preferred_element_type=jnp.float32)
    imag = imag + jnp.einsum("iok,ik->ok", weight[1], modes[0], preferred_element_type=jnp.float32)
    return jnp.stack([real, imag]).astype(jnp.bfloat16)


def on_device_plain(field, cotangent, mode_weight, skip_weight, lift_weight, proj_weight):
    chans, xrows, yrows, zlen = field.shape
    groups_x = lax.axis_size("gx")
    groups_y = lax.axis_size("gy")
    groups_c = lax.axis_size("col")
    span_x = xrows * groups_x
    span_y = yrows * groups_y * groups_c
    column = jnp.arange(MZ, dtype=jnp.int32)
    z_table = real_table(column, zlen)
    y_table = complex_table(centered(MY), span_y)
    x_table = complex_table(centered(MX), span_x).reshape(2, groups_x, xrows, 2, MX)
    tables = (z_table, y_table, x_table)
    local_modes = (mode_weight.shape[3], mode_weight.shape[4], mode_weight.shape[5])
    weight_flat = mode_weight.reshape(2, chans, chans, -1)
    modes = to_modes(field, tables)
    spectral = to_grid(mix(weight_flat, modes), tables, field.shape, local_modes).reshape(chans, -1)
    flat_field = field.reshape(chans, -1)
    flat_grad = cotangent.reshape(chans, -1)
    pre = spectral + jnp.dot(skip_weight, flat_field, preferred_element_type=jnp.float32)
    lifted, slope_pre = gelu_slope(pre)
    lifted = lifted.astype(jnp.bfloat16)
    hidden = jnp.dot(lift_weight, lifted, preferred_element_type=jnp.float32)
    activated, slope_hid = gelu_slope(hidden)
    activated = activated.astype(jnp.bfloat16)
    back_hidden = jnp.dot(proj_weight.T, flat_grad, preferred_element_type=jnp.float32)
    hidden_grad = (back_hidden * slope_hid).astype(jnp.bfloat16)
    grad_up = flat_grad.astype(jnp.float32) + jnp.dot(
        lift_weight.T, hidden_grad, preferred_element_type=jnp.float32
    )
    pre_grad = (grad_up * slope_pre).astype(jnp.bfloat16)
    proj_part = jnp.einsum("cr,hr->ch", flat_grad, activated, preferred_element_type=jnp.float32)
    lift_part = jnp.einsum("hr,cr->hc", hidden_grad, lifted, preferred_element_type=jnp.float32)
    skip_part = jnp.einsum("or,ir->oi", pre_grad, flat_field, preferred_element_type=jnp.float32)
    proj_grad, lift_grad, skip_grad = lax.psum(
        (proj_part, lift_part, skip_part), ("gx", "gy", "col")
    )
    pre_modes = to_modes(pre_grad.reshape(field.shape), tables)
    grad_real = jnp.einsum("ik,ok->iok", modes[0], pre_modes[0], preferred_element_type=jnp.float32)
    grad_real = grad_real + jnp.einsum(
        "ik,ok->iok", modes[1], pre_modes[1], preferred_element_type=jnp.float32
    )
    grad_imag = jnp.einsum("ik,ok->iok", modes[0], pre_modes[1], preferred_element_type=jnp.float32)
    grad_imag = grad_imag - jnp.einsum(
        "ik,ok->iok", modes[1], pre_modes[0], preferred_element_type=jnp.float32
    )
    mode_grad = jnp.stack([grad_real, grad_imag]).astype(jnp.bfloat16).reshape(mode_weight.shape)
    back_real = jnp.einsum(
        "iok,ok->ik", weight_flat[0], pre_modes[0], preferred_element_type=jnp.float32
    )
    back_real = back_real + jnp.einsum(
        "iok,ok->ik", weight_flat[1], pre_modes[1], preferred_element_type=jnp.float32
    )
    back_imag = jnp.einsum(
        "iok,ok->ik", weight_flat[0], pre_modes[1], preferred_element_type=jnp.float32
    )
    back_imag = back_imag - jnp.einsum(
        "iok,ok->ik", weight_flat[1], pre_modes[0], preferred_element_type=jnp.float32
    )
    modes_grad = jnp.stack([back_real, back_imag]).astype(jnp.bfloat16)
    spectral_grad = to_grid(modes_grad, tables, field.shape, local_modes).reshape(chans, -1)
    skip_back = jnp.dot(skip_weight.T, pre_grad, preferred_element_type=jnp.float32)
    field_grad = (spectral_grad + skip_back).astype(jnp.bfloat16).reshape(field.shape)
    return (field_grad, mode_grad, skip_grad, lift_grad, proj_grad)


F32 = jnp.float32
BF16 = jnp.bfloat16
LANES = 128


def np_trig(freqs, length):
    turns = (np.arange(length)[:, None] * (freqs[None, :] % length)) % length
    angle = turns.astype(np.float32) * np.float32(2.0 * math.pi / length)
    factor = np.float32(1.0 / math.sqrt(length))
    return (np.cos(angle) * factor, np.sin(angle) * factor)


def np_complex(freqs, length):
    cosine, sine = np_trig(freqs, length)
    upper = np.stack([cosine, -sine], axis=1)
    lower = np.stack([sine, cosine], axis=1)
    return np.stack([upper, lower])


def host_tables(zlen, yrows, xrows, n_z, n_y, half):
    cosine, sine = np_trig(np.arange(MZ), zlen)
    z_pair = np.stack([cosine.T, -sine.T], axis=1).reshape(2 * MZ, zlen)
    y_full = np_complex(np.arange(MY) - MY // 2, yrows * n_z)
    kyb = MY // n_y
    y_six = y_full.reshape(2, n_z, yrows, 2, n_y, kyb)
    y_fwd = y_six.transpose(4, 3, 5, 1, 0, 2).reshape(2 * MY, 2 * yrows * n_z)
    y_inv = y_six.transpose(1, 0, 2, 4, 3, 5).reshape(2 * yrows * n_z, 2 * MY)
    x_full = np_complex(np.arange(MX) - MX // 2, xrows * n_y).reshape(2, n_y, xrows, 2, MX)
    x_rows = x_full.transpose(1, 0, 2, 3, 4).reshape(n_y, 2, xrows, 1, 2 * MX)
    x_rows = np.broadcast_to(x_rows, (n_y, 2, xrows, half, 2 * MX)).reshape(-1, 2 * MX)
    x_fwd = np.concatenate([x_rows, x_rows], axis=1)
    x_cols = x_full.transpose(3, 4, 1, 0, 2).reshape(2 * MX, n_y, 2, xrows, 1)
    x_inv = np.broadcast_to(x_cols, (2 * MX, n_y, 2, xrows, half)).reshape(2 * MX, -1)
    return [
        jnp.asarray(np.ascontiguousarray(table), BF16)
        for table in (z_pair, y_fwd, y_inv, x_fwd, x_inv)
    ]


def dot(left, right, dims=((1,), (0,))):
    return lax.dot_general(left, right, (dims, ((), ())), preferred_element_type=F32)


NT = ((1,), (1,))
TN = ((0,), (0,))


def gelu_pair(value):
    square = value * value
    tangent = jnp.tanh(value * (KAPPA + (KAPPA * CUBIC) * square))
    half = 0.5 + 0.5 * tangent
    result = value * half
    slope = half + result * (1.0 - tangent) * (KAPPA + (3.0 * KAPPA * CUBIC) * square)
    return (result, slope)


def layer_kernel(
    geo, field_ref, cot_ref, weight_ref, skip_ref, lift_ref, proj_ref,
    tz_ref, tyf_ref, tyi_ref, txf_ref, txi_ref,
    grad_ref, modes_out, premodes_out, sums_out,
    held, packed, dense, cells, cots, cot_in, pgrad, kxf, kxi, spec_grid, mixed, spread,
    modes_ref, premodes_ref, up, send_z, recv_z, send_y, recv_y, sums, sums_x, sums_z,
    weight_sem, own_sem, send_sem, recv_sem, io_sem,
):
    n_gy, n_col, n_y, chans, xrows, yrows, kzb, kyb = geo
    n_z = n_gy * n_col
    half = LANES // xrows
    parts = chans // half
    zlen = cells.shape[-1]
    my_gy, my_col, my_gx = lax.axis_index("gy"), lax.axis_index("col"), lax.axis_index("gx")
    me_z, me_y = my_gy * n_col + my_col, my_gx

    folds = LANES // MX
    fold_rows = kzb * kyb // folds
    loads = weight_sem.shape[0]
    load_chans = chans // loads

    def weight_load(index):
        span = pl.ds(index * load_chans, load_chans)
        return pltpu.make_async_copy(
            weight_ref.at[:, span], held.at[:, span], weight_sem.at[index]
        )

    cot_load = pltpu.make_async_copy(cot_ref, cot_in, io_sem.at[0])
    cot_load.start()
    def load_ahead(first, last):
        for index in range(first, min(last, loads)):
            weight_load(index).start()

    load_ahead(0, 2)

    def fold(tall):
        return jnp.concatenate(
            [tall[at * fold_rows:(at + 1) * fold_rows] for at in range(folds)], axis=1
        )

    block_of = lax.broadcasted_iota(jnp.int32, (fold_rows, LANES), 1) // MX

    def shifts(tiles):
        return [
            [tile] + [pltpu.roll(tile, step * MX, 1) for step in range(1, folds)] for tile in tiles
        ]

    def swap_blocks(moved):
        swapped = []
        for lane in range(folds):
            total = moved[0][-lane % folds]
            for row in range(1, folds):
                total = jnp.where(block_of == row, moved[row][(row - lane) % folds], total)
            swapped.append(total)
        return swapped

    def pack_weight(index):
        weight_load(index).wait()
        outs = 8

        def body(block, carry):
            first = block * outs
            for chan in range(index * load_chans, (index + 1) * load_chans):
                for piece in range(2):
                    for out in range(outs):
                        packed[piece, chan, first + out] = fold(held[piece, chan, first + out])
            return carry

        lax.fori_loop(0, chans // outs, body, 0)

    def peer_z(step):
        other = lax.rem(me_z + step, n_z)
        return other, {"gy": other // n_col, "col": lax.rem(other, n_col)}

    def peer_y(step):
        other = lax.rem(me_y + step, n_y)
        return other, {"gx": other}

    barrier = pltpu.get_barrier_semaphore()
    for step in range(1, n_z):
        pl.semaphore_signal(
            barrier, inc=1, device_id=peer_z(step)[1], device_id_type=pl.DeviceIdType.MESH
        )
    for step in range(1, n_y):
        pl.semaphore_signal(
            barrier, inc=1, device_id=peer_y(step)[1], device_id_type=pl.DeviceIdType.MESH
        )

    def exchange(slot, send, recv, count, me, peer):
        copies = []
        for step in range(1, count):
            other, where = peer(step)
            copy = pltpu.make_async_remote_copy(
                src_ref=send.at[other],
                dst_ref=recv.at[me],
                send_sem=send_sem.at[slot, step],
                recv_sem=recv_sem.at[slot, step],
                device_id=where,
                device_id_type=pl.DeviceIdType.MESH,
            )
            copy.start()
            copies.append(copy)
        own = pltpu.make_async_copy(send.at[me], recv.at[me], own_sem.at[slot])
        own.start()
        copies.append(own)
        return copies

    def exchange_z(phase, part):
        return exchange(
            2 * phase * parts + part, send_z.at[part], recv_z.at[phase, part],
            n_z, me_z, peer_z,
        )

    def exchange_y(phase, part):
        return exchange(
            (2 * phase + 1) * parts + part, send_y.at[part], recv_y.at[phase, part],
            n_y, me_y, peer_y,
        )

    def finish(copies):
        for copy in copies:
            copy.wait()

    def cells_first(source, target):
        for cell in range(xrows):
            rows = source[:, cell, :, :].astype(F32)
            target[:, cell] = jnp.transpose(rows, (1, 0, 2)).astype(BF16)

    def chans_of(part):
        return slice(part * half, (part + 1) * half)

    def start_z(source, phase, part):
        planes = [
            dot(tz_ref[...], source[row, :, chans_of(part), :].reshape(LANES, zlen), NT)
            for row in range(yrows)
        ]
        turned = jnp.transpose(jnp.stack(planes), (1, 0, 2))
        turned = turned.reshape(n_z, kzb, 2 * yrows, LANES).astype(BF16)
        for block in range(n_z):
            send_z[part, block] = jnp.concatenate(
                [turned[block, freq] for freq in range(kzb)], axis=1
            )
        return exchange_z(phase, part)

    def start_y(phase, part):
        rows = recv_z[phase, part].reshape(n_z * 2 * yrows, kzb * LANES)
        moved = dot(tyf_ref[...], rows).astype(BF16)
        send_y[part] = moved.reshape(n_y, 2 * kyb, kzb * LANES)
        return exchange_y(phase, part)

    def reach_modes(phase, part, target):
        blocks = [recv_y[phase, part, group].astype(F32) for group in range(n_y)]
        columns = []
        for group in range(n_y):
            for piece in range(2):
                tiles = [
                    blocks[group][
                        piece * kyb:(piece + 1) * kyb, freq * LANES:(freq + 1) * LANES
                    ]
                    for freq in range(kzb)
                ]
                columns.append(jnp.concatenate(tiles, axis=0).astype(BF16))
        result = dot(jnp.concatenate(columns, axis=1), kxf[...])
        for tile in range(half * 2 * MX // LANES):
            tiles = [
                result[row * fold_rows:(row + 1) * fold_rows, tile * LANES:(tile + 1) * LANES]
                for row in range(folds)
            ]
            moved = shifts(tiles)
            swapped = swap_blocks(moved)
            for lane in range(folds):
                chan, piece = divmod(tile * folds + lane, 2)
                dense[piece, part * half + chan] = swapped[lane].astype(BF16)
                for row in range(folds):
                    target[
                        piece, part * half + chan, row * fold_rows:(row + 1) * fold_rows, :
                    ] = moved[row][-lane % folds][:, :MX].astype(BF16)

    run = 4

    def mix(summed_part, out_part):
        def body(index, carry):
            at = summed_part * half + index * run
            real = [dense[0, at + step] for step in range(run)]
            imag = [dense[1, at + step] for step in range(run)]
            for out in range(out_part * half, (out_part + 1) * half):
                short = [None, None]
                for step in range(run):
                    w_real, w_imag = packed[0, at + step, out], packed[1, at + step, out]
                    new = (
                        w_real * real[step] - w_imag * imag[step],
                        w_real * imag[step] + w_imag * real[step],
                    )
                    for piece in range(2):
                        old = short[piece]
                        short[piece] = new[piece] if old is None else old + new[piece]
                for piece in range(2):
                    mixed[piece, out] += short[piece].astype(F32)
            return carry

        lax.fori_loop(0, half // run, body, 0)

    def mix_back(summed_part, out_part):
        outs = 4

        def body(index, carry):
            first = out_part * half + index * outs
            total = [[mixed[piece, first + out] for piece in range(2)] for out in range(outs)]
            short = [[None, None] for _ in range(outs)]
            for step in range(half):
                summed = summed_part * half + step
                real, imag = dense[0, summed], dense[1, summed]
                for out in range(outs):
                    w_real, w_imag = packed[0, first + out, summed], packed[1, first + out, summed]
                    new = (w_real * real + w_imag * imag, w_real * imag - w_imag * real)
                    for piece in range(2):
                        old = short[out][piece]
                        short[out][piece] = new[piece] if old is None else old + new[piece]
                        if (step + 1) % run == 0:
                            total[out][piece] = total[out][piece] + short[out][piece].astype(F32)
                            short[out][piece] = None
            for out in range(outs):
                for piece in range(2):
                    mixed[piece, first + out] = total[out][piece]
            return carry

        lax.fori_loop(0, half // outs, body, 0)

    def start_back_x(phase, part):
        for tile in range(half * 2 * MX // LANES):
            tiles = []
            for lane in range(folds):
                chan, piece = divmod(tile * folds + lane, 2)
                tiles.append(mixed[piece, part * half + chan])
            swapped = swap_blocks(shifts(tiles))
            for row in range(folds):
                spread[
                    part, row * fold_rows:(row + 1) * fold_rows, tile * LANES:(tile + 1) * LANES
                ] = swapped[row].astype(BF16)
        both = dot(spread[part], kxi[...])
        for group in range(n_y):
            rows = []
            for piece in range(2):
                at = (group * 2 + piece) * LANES
                rows.append(jnp.concatenate(
                    [both[freq * kyb:(freq + 1) * kyb, at:at + LANES] for freq in range(kzb)],
                    axis=1,
                ))
            send_y[part, group] = jnp.concatenate(rows, axis=0).astype(BF16)
        return exchange_y(phase, part)

    def start_back_y(phase, part):
        rows = recv_y[phase, part].reshape(n_y * 2 * kyb, kzb * LANES)
        moved = dot(tyi_ref[...], rows).astype(BF16)
        send_z[part] = moved.reshape(n_z, 2 * yrows, kzb * LANES)
        return exchange_z(phase, part)

    def reach_grid(phase, part, emit):
        tiles = []
        for block in range(n_z):
            rows = recv_z[phase, part, block].astype(F32)
            for freq in range(kzb):
                for piece in range(2):
                    tiles.append(
                        rows[piece * yrows:(piece + 1) * yrows, freq * LANES:(freq + 1) * LANES]
                    )
        turned = jnp.transpose(jnp.stack(tiles), (1, 0, 2)).astype(BF16)
        for row in range(yrows):
            emit(row, part, dot(turned[row], tz_ref[...], TN).reshape(xrows, half, zlen))

    def keep_grid(row, part, values):
        spec_grid[row, :, chans_of(part), :] += values

    def keep_grad(row, part, values):
        total = values + spec_grid[row, :, chans_of(part), :]
        grad_ref[row, :, chans_of(part), :] = total.astype(BF16)

    def wide_cells(ref, row):
        return jnp.concatenate([ref[row, cell] for cell in range(xrows)], axis=1)

    def build_x_tables():
        tall, wide = kxf.shape
        lane = lax.broadcasted_iota(jnp.int32, (tall, LANES), 1)
        line = lax.broadcasted_iota(jnp.int32, (tall, LANES), 0)
        owner = line % half
        pair = txf_ref[...].astype(F32)
        per_tile = LANES // (2 * MX)
        for tile in range(wide // LANES):
            keep = owner == tile * per_tile + lane // (2 * MX)
            kxf[:, tile * LANES:(tile + 1) * LANES] = jnp.where(keep, pair, 0.0).astype(BF16)
        flat = txi_ref[...].astype(F32)
        lane_owner = lax.broadcasted_iota(jnp.int32, flat.shape, 1) % half
        for chan in range(half):
            kxi[chan * 2 * MX:(chan + 1) * 2 * MX, :] = jnp.where(
                lane_owner == chan, flat, 0.0
            ).astype(BF16)

    def prepare(row, carry):
        up[row] = dot(proj_ref[...], wide_cells(cots, row), TN).astype(BF16)
        total = dot(skip_ref[...], wide_cells(cells, row))
        for cell in range(xrows):
            spec_grid[row, cell] = total[:, cell * zlen:(cell + 1) * zlen]
        return carry

    both = range(parts)
    clear = jnp.zeros(mixed.shape, F32)
    cells_first(field_ref, cells)
    load_ahead(2, 4)
    pl.semaphore_wait(barrier, n_z - 1 + n_y - 1)
    going_z = [start_z(cells, 0, part) for part in both]
    load_ahead(4, 5)
    build_x_tables()
    mixed[...] = clear
    load_ahead(5, 6)
    cot_load.wait()
    cells_first(cot_in, cots)
    early = loads // 4
    for index in range(early):
        pack_weight(index)
        load_ahead(6 + index, 7 + index)
    going_y = []
    for part in both:
        finish(going_z[part])
        going_y.append(start_y(0, part))
    for index in range(early, loads):
        pack_weight(index)
    for part in both:
        finish(going_y[part])
        reach_modes(0, part, modes_ref)
        if part < parts - 1:
            for out_part in both:
                mix(part, out_part)
    modes_save = pltpu.make_async_copy(modes_ref, modes_out, io_sem.at[1])
    modes_save.start()
    going_y = []
    for part in both:
        mix(parts - 1, part)
        going_y.append(start_back_x(1, part))
    lax.fori_loop(0, yrows, prepare, 0)
    going_z = []
    for part in both:
        finish(going_y[part])
        going_z.append(start_back_y(1, part))
    sums[...] = jnp.zeros(sums.shape, F32)
    mixed[...] = clear
    for part in both:
        finish(going_z[part])
        reach_grid(1, part, keep_grid)

    pair = 2

    def pointwise(step, carry):
        lines = [step * pair + line for line in range(pair)]
        values = jnp.concatenate([wide_cells(cells, row) for row in lines], axis=1)
        grads = jnp.concatenate([wide_cells(cots, row) for row in lines], axis=1)
        pre = jnp.concatenate(
            [spec_grid[row, cell] for row in lines for cell in range(xrows)], axis=1
        )
        lifted, slope_pre = gelu_pair(pre)
        lifted = lifted.astype(BF16)
        hidden = dot(lift_ref[...], lifted, TN)
        activated, slope_hid = gelu_pair(hidden)
        activated = activated.astype(BF16)
        above = jnp.concatenate([up[row] for row in lines], axis=1).astype(F32)
        hidden_grad = (above * slope_hid).astype(BF16)
        grad_up = grads.astype(F32) + dot(lift_ref[...], hidden_grad)
        pre_grad = (grad_up * slope_pre).astype(BF16)
        sums[0:chans] += dot(grads, activated, NT)
        sums[chans:2 * chans] += dot(lifted, hidden_grad, NT)
        sums[2 * chans:, 0:chans] += dot(pre_grad, values, NT)
        for line in range(pair):
            for cell in range(xrows):
                at = (line * xrows + cell) * zlen
                pgrad[lines[line], cell] = pre_grad[:, at:at + zlen]
        return carry

    lax.fori_loop(0, yrows // pair, pointwise, 0)

    share = sums.shape[0] // n_y
    spare = 8 * parts

    def send_sums(slot, count, me, peer, source, target):
        copies = []
        for step in range(1, count):
            other, where = peer(step)
            copy = pltpu.make_async_remote_copy(
                src_ref=source(other),
                dst_ref=target.at[me],
                send_sem=send_sem.at[slot, step],
                recv_sem=recv_sem.at[slot, step],
                device_id=where,
                device_id_type=pl.DeviceIdType.MESH,
            )
            copy.start()
            copies.append(copy)
        return copies

    def rows_of(index):
        return pl.ds(pl.multiple_of(index * share, 8), share)

    def skip_back(row, carry):
        total = dot(skip_ref[...], wide_cells(pgrad, row), TN)
        for cell in range(xrows):
            spec_grid[row, cell] = total[:, cell * zlen:(cell + 1) * zlen]
        return carry

    going_z = [start_z(pgrad, 2, part) for part in both]
    sums_x[me_y] = sums[rows_of(me_y), :]
    small = send_sums(spare, n_y, me_y, peer_y, lambda other: sums.at[rows_of(other)], sums_x)
    going_y = []
    for part in both:
        finish(going_z[part])
        going_y.append(start_y(2, part))
    finish(small)
    sums_z[me_z] = jnp.sum(sums_x[...], axis=0)
    small = send_sums(spare + 1, n_z, me_z, peer_z, lambda other: sums_z.at[me_z], sums_z)
    lax.fori_loop(0, yrows, skip_back, 0)
    for part in both:
        finish(going_y[part])
        reach_modes(2, part, premodes_ref)
        if part < parts - 1:
            for out_part in both:
                mix_back(part, out_part)
    premodes_save = pltpu.make_async_copy(premodes_ref, premodes_out, io_sem.at[2])
    premodes_save.start()
    going_y = []
    for part in both:
        mix_back(parts - 1, part)
        going_y.append(start_back_x(3, part))
    finish(small)
    sums_out[me_y] = jnp.sum(sums_z[...], axis=0)
    small = send_sums(spare + 2, n_y, me_y, peer_y, lambda other: sums_out.at[me_y], sums_out)
    going_z = []
    for part in both:
        finish(going_y[part])
        going_z.append(start_back_y(3, part))
    finish(small)
    modes_save.wait()
    premodes_save.wait()
    for part in both:
        finish(going_z[part])
        reach_grid(3, part, keep_grad)


def outer_kernel(
    modes_ref, pre_ref, grid_ref, sums_ref, out_ref, field_ref, proj_ref, lift_ref, skip_ref,
    held, grid, turned, out_sem, io_sem,
):
    chans, rows = pre_ref.shape[1], pre_ref.shape[2]
    count = out_sem.shape[0]
    group = chans // count

    grid_load = pltpu.make_async_copy(grid_ref, grid, io_sem.at[0])
    grid_load.start()

    def save(index):
        span = pl.ds(index * group, group)
        return pltpu.make_async_copy(held.at[:, span], out_ref.at[:, span], out_sem.at[index])

    def outer(index, carry):
        first = index * group
        outs = 4

        def body(block, inner):
            for top in range(0, rows, 16):
                m_real = [modes_ref[0, first + chan, top:top + 16] for chan in range(group)]
                m_imag = [modes_ref[1, first + chan, top:top + 16] for chan in range(group)]
                for step in range(outs):
                    out = block * outs + step
                    p_real, p_imag = pre_ref[0, out, top:top + 16], pre_ref[1, out, top:top + 16]
                    for chan in range(group):
                        real = m_real[chan] * p_real + m_imag[chan] * p_imag
                        imag = m_real[chan] * p_imag - m_imag[chan] * p_real
                        held[0, first + chan, out, top:top + 16] = real
                        held[1, first + chan, out, top:top + 16] = imag
            return inner

        lax.fori_loop(0, chans // outs, body, 0)
        save(index).start()
        return carry

    lax.fori_loop(0, count, outer, 0)
    grid_load.wait()
    for cell in range(grid.shape[1]):
        turned[:, cell] = jnp.transpose(grid[:, cell].astype(F32), (1, 0, 2)).astype(BF16)
    field_save = pltpu.make_async_copy(turned, field_ref, io_sem.at[1])
    field_save.start()
    proj_ref[...] = sums_ref[0:chans]
    lift_ref[...] = sums_ref[chans:2 * chans]
    skip_ref[...] = sums_ref[2 * chans:, 0:chans]

    def done(index, carry):
        save(index).wait()
        return carry

    lax.fori_loop(0, count, done, 0)
    field_save.wait()


def finish_gradients(modes, pre_modes, grid, sums):
    _, chans, rows, lanes = modes.shape
    yrows, xrows, _, zlen = grid.shape
    whole = (2, chans, chans, rows, lanes)
    field_shape = (chans, xrows, yrows, zlen)
    vmem = pl.BlockSpec(memory_space=pltpu.VMEM)
    hbm = pl.BlockSpec(memory_space=pl.ANY)
    return pl.pallas_call(
        outer_kernel,
        in_specs=[vmem, vmem, hbm, vmem],
        out_specs=[hbm, hbm, vmem, vmem, vmem],
        out_shape=(
            jax.ShapeDtypeStruct(whole, BF16),
            jax.ShapeDtypeStruct(field_shape, BF16),
            jax.ShapeDtypeStruct((chans, LANES), F32),
            jax.ShapeDtypeStruct((chans, LANES), F32),
            jax.ShapeDtypeStruct((chans, chans), F32),
        ),
        scratch_shapes=[
            pltpu.VMEM(whole, BF16),
            pltpu.VMEM(grid.shape, BF16),
            pltpu.VMEM(field_shape, BF16),
            pltpu.SemaphoreType.DMA((chans // 2,)),
            pltpu.SemaphoreType.DMA((2,)),
        ],
        compiler_params=pltpu.CompilerParams(vmem_limit_bytes=60 << 20),
        name="mode_outer",
    )(modes, pre_modes, grid, sums)


def on_device(field, cotangent, mode_weight, skip_weight, lift_weight, proj_weight):
    chans, xrows, yrows, zlen = field.shape
    kzb, kyb = mode_weight.shape[3], mode_weight.shape[4]
    n_gy, n_col, n_y = lax.axis_size("gy"), lax.axis_size("col"), lax.axis_size("gx")
    n_z = n_gy * n_col
    fits = kyb == 8 and kzb % 2 == 0 and xrows == 8 and yrows == 8 and zlen == LANES
    fits = fits and lift_weight.shape[0] == LANES and (3 * chans) % (8 * n_y) == 0 and chans % 8 == 0
    fits = fits and (kzb * kyb * MX) % (16 * LANES) == 0
    if not fits or 2 * MX * 2 != LANES or chans % (LANES // xrows) or LANES // xrows != 16:
        return on_device_plain(
            field, cotangent, mode_weight, skip_weight, lift_weight, proj_weight
        )
    half = LANES // xrows
    parts = chans // half
    rows = kzb * kyb
    tables = host_tables(zlen, yrows, xrows, n_z, n_y, half)
    weight = mode_weight.reshape(2, chans, chans, rows, MX)
    share = 3 * chans // n_y
    vmem = pl.BlockSpec(memory_space=pltpu.VMEM)
    hbm = pl.BlockSpec(memory_space=pl.ANY)
    geo = (n_gy, n_col, n_y, chans, xrows, yrows, kzb, kyb)
    grid_shape = (yrows, xrows, chans, zlen)
    spectral = (2, chans, rows, MX)
    packed = (2, chans, rows * MX // LANES, LANES)
    outs = pl.pallas_call(
        functools.partial(layer_kernel, geo),
        out_shape=(
            jax.ShapeDtypeStruct(grid_shape, BF16),
            jax.ShapeDtypeStruct(spectral, BF16),
            jax.ShapeDtypeStruct(spectral, BF16),
            jax.ShapeDtypeStruct((n_y, share, LANES), F32),
        ),
        in_specs=[vmem, hbm, hbm] + [vmem] * 8,
        out_specs=(vmem, hbm, hbm, vmem),
        scratch_shapes=[
            pltpu.VMEM(weight.shape, BF16),
            pltpu.VMEM((2, chans, chans, rows * MX // LANES, LANES), BF16),
            pltpu.VMEM(packed, BF16),
            pltpu.VMEM(grid_shape, BF16),
            pltpu.VMEM(grid_shape, BF16),
            pltpu.VMEM(cotangent.shape, BF16),
            pltpu.VMEM(grid_shape, BF16),
            pltpu.VMEM((n_y * 2 * LANES, half * 2 * MX), BF16),
            pltpu.VMEM((half * 2 * MX, n_y * 2 * LANES), BF16),
            pltpu.VMEM(grid_shape, F32),
            pltpu.VMEM(packed, F32),
            pltpu.VMEM((parts, rows, half * 2 * MX), BF16),
            pltpu.VMEM(spectral, BF16),
            pltpu.VMEM(spectral, BF16),
            pltpu.VMEM((yrows, lift_weight.shape[0], xrows * zlen), BF16),
            pltpu.VMEM((parts, n_z, 2 * yrows, kzb * LANES), BF16),
            pltpu.VMEM((4, parts, n_z, 2 * yrows, kzb * LANES), BF16),
            pltpu.VMEM((parts, n_y, 2 * kyb, kzb * LANES), BF16),
            pltpu.VMEM((4, parts, n_y, 2 * kyb, kzb * LANES), BF16),
            pltpu.VMEM((n_y * share, LANES), F32),
            pltpu.VMEM((n_y, share, LANES), F32),
            pltpu.VMEM((n_z, share, LANES), F32),
            pltpu.SemaphoreType.DMA((8,)),
            pltpu.SemaphoreType.DMA((8 * parts,)),
            pltpu.SemaphoreType.DMA((8 * parts + 3, max(n_z, n_y))),
            pltpu.SemaphoreType.DMA((8 * parts + 3, max(n_z, n_y))),
            pltpu.SemaphoreType.DMA((3,)),
        ],
        compiler_params=pltpu.CompilerParams(
            collective_id=0, has_side_effects=True, vmem_limit_bytes=62 << 20
        ),
        name="spectral_layer",
    )(field, cotangent, weight, skip_weight, lift_weight.T, proj_weight, *tables)
    grad, modes, pre_modes, sums = outs
    mode_grad, field_grad, proj_grad, lift_turned, skip_grad = finish_gradients(
        modes, pre_modes, grad, sums.reshape(3 * chans, LANES)
    )
    return (field_grad, mode_grad.reshape(mode_weight.shape), skip_grad, lift_turned.T, proj_grad)


def solution(mesh):
    in_specs = (
        P("grp", "gx", ("gy", "col"), None),
        P("grp", "gx", ("gy", "col"), None),
        P(None, None, None, ("gy", "col"), "gx", None),
        P(),
        P(),
        P(),
    )
    out_specs = (
        P("grp", "gx", ("gy", "col"), None),
        P("grp", None, None, ("gy", "col"), "gx", None),
        P("grp", None),
        P("grp", None),
        P("grp", None),
    )
    return jax.shard_map(
        on_device, mesh=mesh, in_specs=in_specs, out_specs=out_specs, check_vma=False
    )
```

```python
import functools
import math

import jax
import jax.numpy as jnp
import numpy as np
from jax import lax
from jax.experimental import pallas as pl
from jax.experimental.pallas import tpu as pltpu
from jax.sharding import PartitionSpec as P

MX = 32
MY = 32
MZ = 32


KAPPA = 0.7978845608028654
CUBIC = 0.044715


def gelu_slope(value):
    inner = KAPPA * (value + CUBIC * value * value * value)
    tangent = jnp.tanh(inner)
    result = 0.5 * value * (1.0 + tangent)
    slope = 0.5 * (1.0 + tangent) + 0.5 * value * (1.0 - tangent * tangent) * KAPPA * (
        1.0 + 3.0 * CUBIC * value * value
    )
    return (result, slope)


def trig_pair(freqs, length):
    positions = jnp.arange(length, dtype=jnp.int32)
    turns = positions[:, None] * (freqs[None, :] % length) % length
    angle = turns.astype(jnp.float32) * (2.0 * math.pi / length)
    factor = 1.0 / math.sqrt(length)
    return (jnp.cos(angle) * factor, jnp.sin(angle) * factor)


def real_table(freqs, length):
    cosine, sine = trig_pair(freqs, length)
    return jnp.stack([cosine.T, -sine.T]).astype(jnp.bfloat16)


def complex_table(freqs, length):
    cosine, sine = trig_pair(freqs, length)
    upper = jnp.stack([cosine, -sine], axis=1)
    lower = jnp.stack([sine, cosine], axis=1)
    return jnp.stack([upper, lower]).astype(jnp.bfloat16)


def centered(count):
    return jnp.arange(count, dtype=jnp.int32) - count // 2


def to_modes(values, tables):
    z_table, y_table, x_table = tables
    chans, xrows, yrows, zlen = values.shape
    first = jnp.einsum("cxyn,qkn->qkycx", values, z_table, preferred_element_type=jnp.float32)
    first = first.astype(jnp.bfloat16).reshape(2, MZ, yrows, chans * xrows)
    moved = lax.all_to_all(first, ("gy", "col"), split_axis=1, concat_axis=2, tiled=True)
    second = jnp.einsum("pkyr,pyqj->qkjr", moved, y_table, preferred_element_type=jnp.float32)
    second = second.astype(jnp.bfloat16)[:, :, :, None, :]
    crossed = lax.all_to_all(second, "gx", split_axis=2, concat_axis=3, tiled=True)
    crossed = crossed.reshape(crossed.shape[:4] + (chans, xrows))
    third = jnp.einsum("pkjgcx,pgxql->qckjl", crossed, x_table, preferred_element_type=jnp.float32)
    return third.astype(jnp.bfloat16).reshape(2, chans, -1)


def to_grid(spec, tables, shape, local_modes):
    z_table, y_table, x_table = tables
    chans, xrows, yrows, zlen = shape
    spec = spec.reshape((2, chans) + local_modes)
    first = jnp.einsum("pckjl,qgxpl->qkjgcx", spec, x_table, preferred_element_type=jnp.float32)
    first = first.astype(jnp.bfloat16)
    first = first.reshape(first.shape[:4] + (chans * xrows,))
    joined = lax.all_to_all(first, "gx", split_axis=3, concat_axis=2, tiled=True)
    joined = joined.reshape(joined.shape[:3] + (chans * xrows,))
    second = jnp.einsum("pkjr,qypj->qkyr", joined, y_table, preferred_element_type=jnp.float32)
    second = second.astype(jnp.bfloat16)
    returned = lax.all_to_all(second, ("gy", "col"), split_axis=2, concat_axis=1, tiled=True)
    grid = jnp.einsum("pkyr,pkn->ryn", returned, z_table, preferred_element_type=jnp.float32)
    return grid.reshape(chans, xrows, yrows, zlen)


def mix(weight, modes):
    real = jnp.einsum("iok,ik->ok", weight[0], modes[0], preferred_element_type=jnp.float32)
    real = real - jnp.einsum("iok,ik->ok", weight[1], modes[1], preferred_element_type=jnp.float32)
    imag = jnp.einsum("iok,ik->ok", weight[0], modes[1], preferred_element_type=jnp.float32)
    imag = imag + jnp.einsum("iok,ik->ok", weight[1], modes[0], preferred_element_type=jnp.float32)
    return jnp.stack([real, imag]).astype(jnp.bfloat16)


def on_device_plain(field, cotangent, mode_weight, skip_weight, lift_weight, proj_weight):
    chans, xrows, yrows, zlen = field.shape
    groups_x = lax.axis_size("gx")
    groups_y = lax.axis_size("gy")
    groups_c = lax.axis_size("col")
    span_x = xrows * groups_x
    span_y = yrows * groups_y * groups_c
    column = jnp.arange(MZ, dtype=jnp.int32)
    z_table = real_table(column, zlen)
    y_table = complex_table(centered(MY), span_y)
    x_table = complex_table(centered(MX), span_x).reshape(2, groups_x, xrows, 2, MX)
    tables = (z_table, y_table, x_table)
    local_modes = (mode_weight.shape[3], mode_weight.shape[4], mode_weight.shape[5])
    weight_flat = mode_weight.reshape(2, chans, chans, -1)
    modes = to_modes(field, tables)
    spectral = to_grid(mix(weight_flat, modes), tables, field.shape, local_modes).reshape(chans, -1)
    flat_field = field.reshape(chans, -1)
    flat_grad = cotangent.reshape(chans, -1)
    pre = spectral + jnp.dot(skip_weight, flat_field, preferred_element_type=jnp.float32)
    lifted, slope_pre = gelu_slope(pre)
    lifted = lifted.astype(jnp.bfloat16)
    hidden = jnp.dot(lift_weight, lifted, preferred_element_type=jnp.float32)
    activated, slope_hid = gelu_slope(hidden)
    activated = activated.astype(jnp.bfloat16)
    back_hidden = jnp.dot(proj_weight.T, flat_grad, preferred_element_type=jnp.float32)
    hidden_grad = (back_hidden * slope_hid).astype(jnp.bfloat16)
    grad_up = flat_grad.astype(jnp.float32) + jnp.dot(
        lift_weight.T, hidden_grad, preferred_element_type=jnp.float32
    )
    pre_grad = (grad_up * slope_pre).astype(jnp.bfloat16)
    proj_part = jnp.einsum("cr,hr->ch", flat_grad, activated, preferred_element_type=jnp.float32)
    lift_part = jnp.einsum("hr,cr->hc", hidden_grad, lifted, preferred_element_type=jnp.float32)
    skip_part = jnp.einsum("or,ir->oi", pre_grad, flat_field, preferred_element_type=jnp.float32)
    proj_grad, lift_grad, skip_grad = lax.psum(
        (proj_part, lift_part, skip_part), ("gx", "gy", "col")
    )
    pre_modes = to_modes(pre_grad.reshape(field.shape), tables)
    grad_real = jnp.einsum("ik,ok->iok", modes[0], pre_modes[0], preferred_element_type=jnp.float32)
    grad_real = grad_real + jnp.einsum(
        "ik,ok->iok", modes[1], pre_modes[1], preferred_element_type=jnp.float32
    )
    grad_imag = jnp.einsum("ik,ok->iok", modes[0], pre_modes[1], preferred_element_type=jnp.float32)
    grad_imag = grad_imag - jnp.einsum(
        "ik,ok->iok", modes[1], pre_modes[0], preferred_element_type=jnp.float32
    )
    mode_grad = jnp.stack([grad_real, grad_imag]).astype(jnp.bfloat16).reshape(mode_weight.shape)
    back_real = jnp.einsum(
        "iok,ok->ik", weight_flat[0], pre_modes[0], preferred_element_type=jnp.float32
    )
    back_real = back_real + jnp.einsum(
        "iok,ok->ik", weight_flat[1], pre_modes[1], preferred_element_type=jnp.float32
    )
    back_imag = jnp.einsum(
        "iok,ok->ik", weight_flat[0], pre_modes[1], preferred_element_type=jnp.float32
    )
    back_imag = back_imag - jnp.einsum(
        "iok,ok->ik", weight_flat[1], pre_modes[0], preferred_element_type=jnp.float32
    )
    modes_grad = jnp.stack([back_real, back_imag]).astype(jnp.bfloat16)
    spectral_grad = to_grid(modes_grad, tables, field.shape, local_modes).reshape(chans, -1)
    skip_back = jnp.dot(skip_weight.T, pre_grad, preferred_element_type=jnp.float32)
    field_grad = (spectral_grad + skip_back).astype(jnp.bfloat16).reshape(field.shape)
    return (field_grad, mode_grad, skip_grad, lift_grad, proj_grad)


F32 = jnp.float32
BF16 = jnp.bfloat16
LANES = 128


def np_trig(freqs, length):
    turns = (np.arange(length)[:, None] * (freqs[None, :] % length)) % length
    angle = turns.astype(np.float32) * np.float32(2.0 * math.pi / length)
    factor = np.float32(1.0 / math.sqrt(length))
    return (np.cos(angle) * factor, np.sin(angle) * factor)


def np_complex(freqs, length):
    cosine, sine = np_trig(freqs, length)
    upper = np.stack([cosine, -sine], axis=1)
    lower = np.stack([sine, cosine], axis=1)
    return np.stack([upper, lower])


def host_tables(zlen, yrows, xrows, n_z, n_y, half):
    cosine, sine = np_trig(np.arange(MZ), zlen)
    z_pair = np.stack([cosine.T, -sine.T], axis=1).reshape(2 * MZ, zlen)
    y_full = np_complex(np.arange(MY) - MY // 2, yrows * n_z)
    kyb = MY // n_y
    y_six = y_full.reshape(2, n_z, yrows, 2, n_y, kyb)
    y_fwd = y_six.transpose(4, 3, 5, 1, 0, 2).reshape(2 * MY, 2 * yrows * n_z)
    y_inv = y_six.transpose(1, 0, 2, 4, 3, 5).reshape(2 * yrows * n_z, 2 * MY)
    x_full = np_complex(np.arange(MX) - MX // 2, xrows * n_y).reshape(2, n_y, xrows, 2, MX)
    x_rows = x_full.transpose(1, 0, 2, 3, 4).reshape(n_y, 2, xrows, 1, 2 * MX)
    x_rows = np.broadcast_to(x_rows, (n_y, 2, xrows, half, 2 * MX)).reshape(-1, 2 * MX)
    x_fwd = np.concatenate([x_rows, x_rows], axis=1)
    x_cols = x_full.transpose(3, 4, 1, 0, 2).reshape(2 * MX, n_y, 2, xrows, 1)
    x_inv = np.broadcast_to(x_cols, (2 * MX, n_y, 2, xrows, half)).reshape(2 * MX, -1)
    return [
        jnp.asarray(np.ascontiguousarray(table), BF16)
        for table in (z_pair, y_fwd, y_inv, x_fwd, x_inv)
    ]


def dot(left, right, dims=((1,), (0,))):
    return lax.dot_general(left, right, (dims, ((), ())), preferred_element_type=F32)


NT = ((1,), (1,))
TN = ((0,), (0,))


def gelu_pair(value):
    square = value * value
    tangent = jnp.tanh(value * (KAPPA + (KAPPA * CUBIC) * square))
    half = 0.5 + 0.5 * tangent
    result = value * half
    slope = half + result * (1.0 - tangent) * (KAPPA + (3.0 * KAPPA * CUBIC) * square)
    return (result, slope)


def layer_kernel(
    geo, field_ref, cot_ref, weight_ref, skip_ref, lift_ref, proj_ref,
    tz_ref, tyf_ref, tyi_ref, txf_ref, txi_ref,
    grad_ref, modes_out, premodes_out, sums_out,
    held, packed, dense, cells, cots, cot_in, pgrad, kxf, kxi, spec_grid, mixed, spread,
    modes_ref, premodes_ref, up, send_z, recv_z, send_y, recv_y, sums, sums_x, sums_z,
    weight_sem, own_sem, send_sem, recv_sem, io_sem,
):
    n_gy, n_col, n_y, chans, xrows, yrows, kzb, kyb = geo
    n_z = n_gy * n_col
    half = LANES // xrows
    parts = chans // half
    zlen = cells.shape[-1]
    my_gy, my_col, my_gx = lax.axis_index("gy"), lax.axis_index("col"), lax.axis_index("gx")
    me_z, me_y = my_gy * n_col + my_col, my_gx

    folds = LANES // MX
    fold_rows = kzb * kyb // folds
    loads = weight_sem.shape[0]
    load_chans = chans // loads

    def weight_load(index):
        span = pl.ds(index * load_chans, load_chans)
        return pltpu.make_async_copy(
            weight_ref.at[:, span], held.at[:, span], weight_sem.at[index]
        )

    cot_load = pltpu.make_async_copy(cot_ref, cot_in, io_sem.at[0])
    cot_load.start()
    def load_ahead(first, last):
        for index in range(first, min(last, loads)):
            weight_load(index).start()

    load_ahead(0, 2)

    def fold(tall):
        return jnp.concatenate(
            [tall[at * fold_rows:(at + 1) * fold_rows] for at in range(folds)], axis=1
        )

    block_of = lax.broadcasted_iota(jnp.int32, (fold_rows, LANES), 1) // MX

    def shifts(tiles):
        return [
            [tile] + [pltpu.roll(tile, step * MX, 1) for step in range(1, folds)] for tile in tiles
        ]

    def swap_blocks(moved):
        swapped = []
        for lane in range(folds):
            total = moved[0][-lane % folds]
            for row in range(1, folds):
                total = jnp.where(block_of == row, moved[row][(row - lane) % folds], total)
            swapped.append(total)
        return swapped

    def pack_weight(index):
        weight_load(index).wait()
        outs = 8

        def body(block, carry):
            first = block * outs
            for chan in range(index * load_chans, (index + 1) * load_chans):
                for piece in range(2):
                    for out in range(outs):
                        packed[piece, chan, first + out] = fold(held[piece, chan, first + out])
            return carry

        lax.fori_loop(0, chans // outs, body, 0)

    def peer_z(step):
        other = lax.rem(me_z + step, n_z)
        return other, {"gy": other // n_col, "col": lax.rem(other, n_col)}

    def peer_y(step):
        other = lax.rem(me_y + step, n_y)
        return other, {"gx": other}

    barrier = pltpu.get_barrier_semaphore()
    for step in range(1, n_z):
        pl.semaphore_signal(
            barrier, inc=1, device_id=peer_z(step)[1], device_id_type=pl.DeviceIdType.MESH
        )
    for step in range(1, n_y):
        pl.semaphore_signal(
            barrier, inc=1, device_id=peer_y(step)[1], device_id_type=pl.DeviceIdType.MESH
        )

    def exchange(slot, send, recv, count, me, peer):
        copies = []
        for step in range(1, count):
            other, where = peer(step)
            copy = pltpu.make_async_remote_copy(
                src_ref=send.at[other],
                dst_ref=recv.at[me],
                send_sem=send_sem.at[slot, step],
                recv_sem=recv_sem.at[slot, step],
                device_id=where,
                device_id_type=pl.DeviceIdType.MESH,
            )
            copy.start()
            copies.append(copy)
        own = pltpu.make_async_copy(send.at[me], recv.at[me], own_sem.at[slot])
        own.start()
        copies.append(own)
        return copies

    def exchange_z(phase, part):
        return exchange(
            2 * phase * parts + part, send_z.at[part], recv_z.at[phase, part],
            n_z, me_z, peer_z,
        )

    def exchange_y(phase, part):
        return exchange(
            (2 * phase + 1) * parts + part, send_y.at[part], recv_y.at[phase, part],
            n_y, me_y, peer_y,
        )

    def finish(copies):
        for copy in copies:
            copy.wait()

    def cells_first(source, target):
        for cell in range(xrows):
            rows = source[:, cell, :, :].astype(F32)
            target[:, cell] = jnp.transpose(rows, (1, 0, 2)).astype(BF16)

    def chans_of(part):
        return slice(part * half, (part + 1) * half)

    def start_z(source, phase, part):
        planes = [
            dot(tz_ref[...], source[row, :, chans_of(part), :].reshape(LANES, zlen), NT)
            for row in range(yrows)
        ]
        turned = jnp.transpose(jnp.stack(planes), (1, 0, 2))
        turned = turned.reshape(n_z, kzb, 2 * yrows, LANES).astype(BF16)
        for block in range(n_z):
            send_z[part, block] = jnp.concatenate(
                [turned[block, freq] for freq in range(kzb)], axis=1
            )
        return exchange_z(phase, part)

    def start_y(phase, part):
        rows = recv_z[phase, part].reshape(n_z * 2 * yrows, kzb * LANES)
        moved = dot(tyf_ref[...], rows).astype(BF16)
        send_y[part] = moved.reshape(n_y, 2 * kyb, kzb * LANES)
        return exchange_y(phase, part)

    def reach_modes(phase, part, target):
        blocks = [recv_y[phase, part, group].astype(F32) for group in range(n_y)]
        columns = []
        for group in range(n_y):
            for piece in range(2):
                tiles = [
                    blocks[group][
                        piece * kyb:(piece + 1) * kyb, freq * LANES:(freq + 1) * LANES
                    ]
                    for freq in range(kzb)
                ]
                columns.append(jnp.concatenate(tiles, axis=0).astype(BF16))
        result = dot(jnp.concatenate(columns, axis=1), kxf[...])
        for tile in range(half * 2 * MX // LANES):
            tiles = [
                result[row * fold_rows:(row + 1) * fold_rows, tile * LANES:(tile + 1) * LANES]
                for row in range(folds)
            ]
            moved = shifts(tiles)
            swapped = swap_blocks(moved)
            for lane in range(folds):
                chan, piece = divmod(tile * folds + lane, 2)
                dense[piece, part * half + chan] = swapped[lane].astype(BF16)
                for row in range(folds):
                    target[
                        piece, part * half + chan, row * fold_rows:(row + 1) * fold_rows, :
                    ] = moved[row][-lane % folds][:, :MX].astype(BF16)

    run = 4

    def mix(summed_part, out_part):
        def body(index, carry):
            at = summed_part * half + index * run
            real = [dense[0, at + step] for step in range(run)]
            imag = [dense[1, at + step] for step in range(run)]
            for out in range(out_part * half, (out_part + 1) * half):
                short = [None, None]
                for step in range(run):
                    w_real, w_imag = packed[0, at + step, out], packed[1, at + step, out]
                    new = (
                        w_real * real[step] - w_imag * imag[step],
                        w_real * imag[step] + w_imag * real[step],
                    )
                    for piece in range(2):
                        old = short[piece]
                        short[piece] = new[piece] if old is None else old + new[piece]
                for piece in range(2):
                    mixed[piece, out] += short[piece].astype(F32)
            return carry

        lax.fori_loop(0, half // run, body, 0)

    def mix_back(summed_part, out_part):
        outs = 4

        def body(index, carry):
            first = out_part * half + index * outs
            total = [[mixed[piece, first + out] for piece in range(2)] for out in range(outs)]
            short = [[None, None] for _ in range(outs)]
            for step in range(half):
                summed = summed_part * half + step
                real, imag = dense[0, summed], dense[1, summed]
                for out in range(outs):
                    w_real, w_imag = packed[0, first + out, summed], packed[1, first + out, summed]
                    new = (w_real * real + w_imag * imag, w_real * imag - w_imag * real)
                    for piece in range(2):
                        old = short[out][piece]
                        short[out][piece] = new[piece] if old is None else old + new[piece]
                        if (step + 1) % run == 0:
                            total[out][piece] = total[out][piece] + short[out][piece].astype(F32)
                            short[out][piece] = None
            for out in range(outs):
                for piece in range(2):
                    mixed[piece, first + out] = total[out][piece]
            return carry

        lax.fori_loop(0, half // outs, body, 0)

    def start_back_x(phase, part):
        for tile in range(half * 2 * MX // LANES):
            tiles = []
            for lane in range(folds):
                chan, piece = divmod(tile * folds + lane, 2)
                tiles.append(mixed[piece, part * half + chan])
            swapped = swap_blocks(shifts(tiles))
            for row in range(folds):
                spread[
                    part, row * fold_rows:(row + 1) * fold_rows, tile * LANES:(tile + 1) * LANES
                ] = swapped[row].astype(BF16)
        both = dot(spread[part], kxi[...])
        for group in range(n_y):
            rows = []
            for piece in range(2):
                at = (group * 2 + piece) * LANES
                rows.append(jnp.concatenate(
                    [both[freq * kyb:(freq + 1) * kyb, at:at + LANES] for freq in range(kzb)],
                    axis=1,
                ))
            send_y[part, group] = jnp.concatenate(rows, axis=0).astype(BF16)
        return exchange_y(phase, part)

    def start_back_y(phase, part):
        rows = recv_y[phase, part].reshape(n_y * 2 * kyb, kzb * LANES)
        moved = dot(tyi_ref[...], rows).astype(BF16)
        send_z[part] = moved.reshape(n_z, 2 * yrows, kzb * LANES)
        return exchange_z(phase, part)

    def reach_grid(phase, part, emit):
        tiles = []
        for block in range(n_z):
            rows = recv_z[phase, part, block].astype(F32)
            for freq in range(kzb):
                for piece in range(2):
                    tiles.append(
                        rows[piece * yrows:(piece + 1) * yrows, freq * LANES:(freq + 1) * LANES]
                    )
        turned = jnp.transpose(jnp.stack(tiles), (1, 0, 2)).astype(BF16)
        for row in range(yrows):
            emit(row, part, dot(turned[row], tz_ref[...], TN).reshape(xrows, half, zlen))

    def keep_grid(row, part, values):
        spec_grid[row, :, chans_of(part), :] += values

    def keep_grad(row, part, values):
        total = values + spec_grid[row, :, chans_of(part), :]
        grad_ref[row, :, chans_of(part), :] = total.astype(BF16)

    def wide_cells(ref, row):
        return jnp.concatenate([ref[row, cell] for cell in range(xrows)], axis=1)

    def build_x_tables():
        tall, wide = kxf.shape
        lane = lax.broadcasted_iota(jnp.int32, (tall, LANES), 1)
        line = lax.broadcasted_iota(jnp.int32, (tall, LANES), 0)
        owner = line % half
        pair = txf_ref[...].astype(F32)
        per_tile = LANES // (2 * MX)
        for tile in range(wide // LANES):
            keep = owner == tile * per_tile + lane // (2 * MX)
            kxf[:, tile * LANES:(tile + 1) * LANES] = jnp.where(keep, pair, 0.0).astype(BF16)
        flat = txi_ref[...].astype(F32)
        lane_owner = lax.broadcasted_iota(jnp.int32, flat.shape, 1) % half
        for chan in range(half):
            kxi[chan * 2 * MX:(chan + 1) * 2 * MX, :] = jnp.where(
                lane_owner == chan, flat, 0.0
            ).astype(BF16)

    def prepare(row, carry):
        up[row] = dot(proj_ref[...], wide_cells(cots, row), TN).astype(BF16)
        total = dot(skip_ref[...], wide_cells(cells, row))
        for cell in range(xrows):
            spec_grid[row, cell] = total[:, cell * zlen:(cell + 1) * zlen]
        return carry

    both = range(parts)
    clear = jnp.zeros(mixed.shape, F32)
    cells_first(field_ref, cells)
    load_ahead(2, 4)
    build_x_tables()
    mixed[...] = clear
    pl.semaphore_wait(barrier, n_z - 1 + n_y - 1)
    going_z = [start_z(cells, 0, part) for part in both]
    load_ahead(4, 6)
    early = 3 * loads // 8
    for index in range(early):
        pack_weight(index)
        load_ahead(6 + index, 7 + index)
    going_y = []
    for part in both:
        finish(going_z[part])
        going_y.append(start_y(0, part))
    for index in range(early, loads):
        pack_weight(index)
    for part in both:
        finish(going_y[part])
        reach_modes(0, part, modes_ref)
        if part < parts - 1:
            for out_part in both:
                mix(part, out_part)
    modes_save = pltpu.make_async_copy(modes_ref, modes_out, io_sem.at[1])
    modes_save.start()
    going_y = []
    for part in both:
        mix(parts - 1, part)
        going_y.append(start_back_x(1, part))
    cot_load.wait()
    cells_first(cot_in, cots)
    lax.fori_loop(0, yrows, prepare, 0)
    going_z = []
    for part in both:
        finish(going_y[part])
        going_z.append(start_back_y(1, part))
    sums[...] = jnp.zeros(sums.shape, F32)
    mixed[...] = clear
    for part in both:
        finish(going_z[part])
        reach_grid(1, part, keep_grid)

    pair = 2

    def pointwise(step, carry):
        lines = [step * pair + line for line in range(pair)]
        grads = jnp.concatenate([wide_cells(cots, row) for row in lines], axis=1)
        pre = jnp.concatenate(
            [spec_grid[row, cell] for row in lines for cell in range(xrows)], axis=1
        )
        lifted, slope_pre = gelu_pair(pre)
        lifted = lifted.astype(BF16)
        hidden = dot(lift_ref[...], lifted, TN)
        activated, slope_hid = gelu_pair(hidden)
        activated = activated.astype(BF16)
        above = jnp.concatenate([up[row] for row in lines], axis=1).astype(F32)
        hidden_grad = (above * slope_hid).astype(BF16)
        grad_up = grads.astype(F32) + dot(lift_ref[...], hidden_grad)
        pre_grad = (grad_up * slope_pre).astype(BF16)
        sums[0:chans] += dot(grads, activated, NT)
        for line in range(pair):
            span = xrows * zlen
            up[lines[line]] = hidden_grad[:, line * span:(line + 1) * span]
            for cell in range(xrows):
                at = (line * xrows + cell) * zlen
                pgrad[lines[line], cell] = pre_grad[:, at:at + zlen]
                spec_grid[lines[line], cell] = lifted[:, at:at + zlen].astype(F32)
        return carry

    def late_sums(row, carry):
        lifted = wide_cells(spec_grid, row).astype(BF16)
        sums[chans:2 * chans] += dot(lifted, up[row], NT)
        sums[2 * chans:, 0:chans] += dot(wide_cells(pgrad, row), wide_cells(cells, row), NT)
        return carry

    lax.fori_loop(0, yrows // pair, pointwise, 0)

    share = sums.shape[0] // n_y
    spare = 8 * parts

    def send_sums(slot, count, me, peer, source, target):
        copies = []
        for step in range(1, count):
            other, where = peer(step)
            copy = pltpu.make_async_remote_copy(
                src_ref=source(other),
                dst_ref=target.at[me],
                send_sem=send_sem.at[slot, step],
                recv_sem=recv_sem.at[slot, step],
                device_id=where,
                device_id_type=pl.DeviceIdType.MESH,
            )
            copy.start()
            copies.append(copy)
        return copies

    def rows_of(index):
        return pl.ds(pl.multiple_of(index * share, 8), share)

    def skip_back(row, carry):
        total = dot(skip_ref[...], wide_cells(pgrad, row), TN)
        for cell in range(xrows):
            spec_grid[row, cell] = total[:, cell * zlen:(cell + 1) * zlen]
        return carry

    going_z = [start_z(pgrad, 2, part) for part in both]
    lax.fori_loop(0, yrows, late_sums, 0)
    sums_x[me_y] = sums[rows_of(me_y), :]
    small = send_sums(spare, n_y, me_y, peer_y, lambda other: sums.at[rows_of(other)], sums_x)
    going_y = []
    for part in both:
        finish(going_z[part])
        going_y.append(start_y(2, part))
    lax.fori_loop(0, yrows, skip_back, 0)
    for part in both:
        finish(going_y[part])
        reach_modes(2, part, premodes_ref)
        if part < parts - 1:
            for out_part in both:
                mix_back(part, out_part)
        if part == 0:
            finish(small)
            sums_z[me_z] = jnp.sum(sums_x[...], axis=0)
            small = send_sums(
                spare + 1, n_z, me_z, peer_z, lambda other: sums_z.at[me_z], sums_z
            )
    premodes_save = pltpu.make_async_copy(premodes_ref, premodes_out, io_sem.at[2])
    premodes_save.start()
    going_y = []
    for part in both:
        mix_back(parts - 1, part)
        going_y.append(start_back_x(3, part))
    finish(small)
    sums_out[me_y] = jnp.sum(sums_z[...], axis=0)
    small = send_sums(spare + 2, n_y, me_y, peer_y, lambda other: sums_out.at[me_y], sums_out)
    going_z = []
    for part in both:
        finish(going_y[part])
        going_z.append(start_back_y(3, part))
    finish(small)
    modes_save.wait()
    premodes_save.wait()
    for part in both:
        finish(going_z[part])
        reach_grid(3, part, keep_grad)


def outer_kernel(
    modes_ref, pre_ref, grid_ref, sums_ref, out_ref, field_ref, proj_ref, lift_ref, skip_ref,
    held, grid, turned, out_sem, io_sem,
):
    chans, rows = pre_ref.shape[1], pre_ref.shape[2]
    count = out_sem.shape[0]
    group = chans // count

    grid_load = pltpu.make_async_copy(grid_ref, grid, io_sem.at[0])
    grid_load.start()

    def save(index):
        span = pl.ds(index * group, group)
        return pltpu.make_async_copy(held.at[:, span], out_ref.at[:, span], out_sem.at[index])

    def outer(index, carry):
        first = index * group
        outs = 4

        def body(block, inner):
            for top in range(0, rows, 16):
                m_real = [modes_ref[0, first + chan, top:top + 16] for chan in range(group)]
                m_imag = [modes_ref[1, first + chan, top:top + 16] for chan in range(group)]
                for step in range(outs):
                    out = block * outs + step
                    p_real, p_imag = pre_ref[0, out, top:top + 16], pre_ref[1, out, top:top + 16]
                    for chan in range(group):
                        real = m_real[chan] * p_real + m_imag[chan] * p_imag
                        imag = m_real[chan] * p_imag - m_imag[chan] * p_real
                        held[0, first + chan, out, top:top + 16] = real
                        held[1, first + chan, out, top:top + 16] = imag
            return inner

        lax.fori_loop(0, chans // outs, body, 0)
        save(index).start()
        return carry

    lax.fori_loop(0, count, outer, 0)
    grid_load.wait()
    for cell in range(grid.shape[1]):
        turned[:, cell] = jnp.transpose(grid[:, cell].astype(F32), (1, 0, 2)).astype(BF16)
    field_save = pltpu.make_async_copy(turned, field_ref, io_sem.at[1])
    field_save.start()
    proj_ref[...] = sums_ref[0:chans]
    lift_ref[...] = sums_ref[chans:2 * chans]
    skip_ref[...] = sums_ref[2 * chans:, 0:chans]

    def done(index, carry):
        save(index).wait()
        return carry

    lax.fori_loop(0, count, done, 0)
    field_save.wait()


def finish_gradients(modes, pre_modes, grid, sums):
    _, chans, rows, lanes = modes.shape
    yrows, xrows, _, zlen = grid.shape
    whole = (2, chans, chans, rows, lanes)
    field_shape = (chans, xrows, yrows, zlen)
    vmem = pl.BlockSpec(memory_space=pltpu.VMEM)
    hbm = pl.BlockSpec(memory_space=pl.ANY)
    return pl.pallas_call(
        outer_kernel,
        in_specs=[vmem, vmem, hbm, vmem],
        out_specs=[hbm, hbm, vmem, vmem, vmem],
        out_shape=(
            jax.ShapeDtypeStruct(whole, BF16),
            jax.ShapeDtypeStruct(field_shape, BF16),
            jax.ShapeDtypeStruct((chans, LANES), F32),
            jax.ShapeDtypeStruct((chans, LANES), F32),
            jax.ShapeDtypeStruct((chans, chans), F32),
        ),
        scratch_shapes=[
            pltpu.VMEM(whole, BF16),
            pltpu.VMEM(grid.shape, BF16),
            pltpu.VMEM(field_shape, BF16),
            pltpu.SemaphoreType.DMA((chans // 2,)),
            pltpu.SemaphoreType.DMA((2,)),
        ],
        compiler_params=pltpu.CompilerParams(vmem_limit_bytes=60 << 20),
        name="mode_outer",
    )(modes, pre_modes, grid, sums)


def on_device(field, cotangent, mode_weight, skip_weight, lift_weight, proj_weight):
    chans, xrows, yrows, zlen = field.shape
    kzb, kyb = mode_weight.shape[3], mode_weight.shape[4]
    n_gy, n_col, n_y = lax.axis_size("gy"), lax.axis_size("col"), lax.axis_size("gx")
    n_z = n_gy * n_col
    fits = kyb == 8 and kzb % 2 == 0 and xrows == 8 and yrows == 8 and zlen == LANES
    fits = fits and lift_weight.shape[0] == LANES and (3 * chans) % (8 * n_y) == 0 and chans % 8 == 0
    fits = fits and (kzb * kyb * MX) % (16 * LANES) == 0
    if not fits or 2 * MX * 2 != LANES or chans % (LANES // xrows) or LANES // xrows != 16:
        return on_device_plain(
            field, cotangent, mode_weight, skip_weight, lift_weight, proj_weight
        )
    half = LANES // xrows
    parts = chans // half
    rows = kzb * kyb
    tables = host_tables(zlen, yrows, xrows, n_z, n_y, half)
    weight = mode_weight.reshape(2, chans, chans, rows, MX)
    share = 3 * chans // n_y
    vmem = pl.BlockSpec(memory_space=pltpu.VMEM)
    hbm = pl.BlockSpec(memory_space=pl.ANY)
    geo = (n_gy, n_col, n_y, chans, xrows, yrows, kzb, kyb)
    grid_shape = (yrows, xrows, chans, zlen)
    spectral = (2, chans, rows, MX)
    packed = (2, chans, rows * MX // LANES, LANES)
    outs = pl.pallas_call(
        functools.partial(layer_kernel, geo),
        out_shape=(
            jax.ShapeDtypeStruct(grid_shape, BF16),
            jax.ShapeDtypeStruct(spectral, BF16),
            jax.ShapeDtypeStruct(spectral, BF16),
            jax.ShapeDtypeStruct((n_y, share, LANES), F32),
        ),
        in_specs=[vmem, hbm, hbm] + [vmem] * 8,
        out_specs=(vmem, hbm, hbm, vmem),
        scratch_shapes=[
            pltpu.VMEM(weight.shape, BF16),
            pltpu.VMEM((2, chans, chans, rows * MX // LANES, LANES), BF16),
            pltpu.VMEM(packed, BF16),
            pltpu.VMEM(grid_shape, BF16),
            pltpu.VMEM(grid_shape, BF16),
            pltpu.VMEM(cotangent.shape, BF16),
            pltpu.VMEM(grid_shape, BF16),
            pltpu.VMEM((n_y * 2 * LANES, half * 2 * MX), BF16),
            pltpu.VMEM((half * 2 * MX, n_y * 2 * LANES), BF16),
            pltpu.VMEM(grid_shape, F32),
            pltpu.VMEM(packed, F32),
            pltpu.VMEM((parts, rows, half * 2 * MX), BF16),
            pltpu.VMEM(spectral, BF16),
            pltpu.VMEM(spectral, BF16),
            pltpu.VMEM((yrows, lift_weight.shape[0], xrows * zlen), BF16),
            pltpu.VMEM((parts, n_z, 2 * yrows, kzb * LANES), BF16),
            pltpu.VMEM((4, parts, n_z, 2 * yrows, kzb * LANES), BF16),
            pltpu.VMEM((parts, n_y, 2 * kyb, kzb * LANES), BF16),
            pltpu.VMEM((4, parts, n_y, 2 * kyb, kzb * LANES), BF16),
            pltpu.VMEM((n_y * share, LANES), F32),
            pltpu.VMEM((n_y, share, LANES), F32),
            pltpu.VMEM((n_z, share, LANES), F32),
            pltpu.SemaphoreType.DMA((8,)),
            pltpu.SemaphoreType.DMA((8 * parts,)),
            pltpu.SemaphoreType.DMA((8 * parts + 3, max(n_z, n_y))),
            pltpu.SemaphoreType.DMA((8 * parts + 3, max(n_z, n_y))),
            pltpu.SemaphoreType.DMA((3,)),
        ],
        compiler_params=pltpu.CompilerParams(
            collective_id=0, has_side_effects=True, vmem_limit_bytes=62 << 20
        ),
        name="spectral_layer",
    )(field, cotangent, weight, skip_weight, lift_weight.T, proj_weight, *tables)
    grad, modes, pre_modes, sums = outs
    mode_grad, field_grad, proj_grad, lift_turned, skip_grad = finish_gradients(
        modes, pre_modes, grad, sums.reshape(3 * chans, LANES)
    )
    return (field_grad, mode_grad.reshape(mode_weight.shape), skip_grad, lift_turned.T, proj_grad)


def solution(mesh):
    in_specs = (
        P("grp", "gx", ("gy", "col"), None),
        P("grp", "gx", ("gy", "col"), None),
        P(None, None, None, ("gy", "col"), "gx", None),
        P(),
        P(),
        P(),
    )
    out_specs = (
        P("grp", "gx", ("gy", "col"), None),
        P("grp", None, None, ("gy", "col"), "gx", None),
        P("grp", None),
        P("grp", None),
        P("grp", None),
    )
    return jax.shard_map(
        on_device, mesh=mesh, in_specs=in_specs, out_specs=out_specs, check_vma=False
    )
```

```python
import functools
import math

import jax
import jax.numpy as jnp
import numpy as np
from jax import lax
from jax.experimental import pallas as pl
from jax.experimental.pallas import tpu as pltpu
from jax.sharding import PartitionSpec as P

MX = 32
MY = 32
MZ = 32


KAPPA = 0.7978845608028654
CUBIC = 0.044715


def gelu_slope(value):
    inner = KAPPA * (value + CUBIC * value * value * value)
    tangent = jnp.tanh(inner)
    result = 0.5 * value * (1.0 + tangent)
    slope = 0.5 * (1.0 + tangent) + 0.5 * value * (1.0 - tangent * tangent) * KAPPA * (
        1.0 + 3.0 * CUBIC * value * value
    )
    return (result, slope)


def trig_pair(freqs, length):
    positions = jnp.arange(length, dtype=jnp.int32)
    turns = positions[:, None] * (freqs[None, :] % length) % length
    angle = turns.astype(jnp.float32) * (2.0 * math.pi / length)
    factor = 1.0 / math.sqrt(length)
    return (jnp.cos(angle) * factor, jnp.sin(angle) * factor)


def real_table(freqs, length):
    cosine, sine = trig_pair(freqs, length)
    return jnp.stack([cosine.T, -sine.T]).astype(jnp.bfloat16)


def complex_table(freqs, length):
    cosine, sine = trig_pair(freqs, length)
    upper = jnp.stack([cosine, -sine], axis=1)
    lower = jnp.stack([sine, cosine], axis=1)
    return jnp.stack([upper, lower]).astype(jnp.bfloat16)


def centered(count):
    return jnp.arange(count, dtype=jnp.int32) - count // 2


def to_modes(values, tables):
    z_table, y_table, x_table = tables
    chans, xrows, yrows, zlen = values.shape
    first = jnp.einsum("cxyn,qkn->qkycx", values, z_table, preferred_element_type=jnp.float32)
    first = first.astype(jnp.bfloat16).reshape(2, MZ, yrows, chans * xrows)
    moved = lax.all_to_all(first, ("gy", "col"), split_axis=1, concat_axis=2, tiled=True)
    second = jnp.einsum("pkyr,pyqj->qkjr", moved, y_table, preferred_element_type=jnp.float32)
    second = second.astype(jnp.bfloat16)[:, :, :, None, :]
    crossed = lax.all_to_all(second, "gx", split_axis=2, concat_axis=3, tiled=True)
    crossed = crossed.reshape(crossed.shape[:4] + (chans, xrows))
    third = jnp.einsum("pkjgcx,pgxql->qckjl", crossed, x_table, preferred_element_type=jnp.float32)
    return third.astype(jnp.bfloat16).reshape(2, chans, -1)


def to_grid(spec, tables, shape, local_modes):
    z_table, y_table, x_table = tables
    chans, xrows, yrows, zlen = shape
    spec = spec.reshape((2, chans) + local_modes)
    first = jnp.einsum("pckjl,qgxpl->qkjgcx", spec, x_table, preferred_element_type=jnp.float32)
    first = first.astype(jnp.bfloat16)
    first = first.reshape(first.shape[:4] + (chans * xrows,))
    joined = lax.all_to_all(first, "gx", split_axis=3, concat_axis=2, tiled=True)
    joined = joined.reshape(joined.shape[:3] + (chans * xrows,))
    second = jnp.einsum("pkjr,qypj->qkyr", joined, y_table, preferred_element_type=jnp.float32)
    second = second.astype(jnp.bfloat16)
    returned = lax.all_to_all(second, ("gy", "col"), split_axis=2, concat_axis=1, tiled=True)
    grid = jnp.einsum("pkyr,pkn->ryn", returned, z_table, preferred_element_type=jnp.float32)
    return grid.reshape(chans, xrows, yrows, zlen)


def mix(weight, modes):
    real = jnp.einsum("iok,ik->ok", weight[0], modes[0], preferred_element_type=jnp.float32)
    real = real - jnp.einsum("iok,ik->ok", weight[1], modes[1], preferred_element_type=jnp.float32)
    imag = jnp.einsum("iok,ik->ok", weight[0], modes[1], preferred_element_type=jnp.float32)
    imag = imag + jnp.einsum("iok,ik->ok", weight[1], modes[0], preferred_element_type=jnp.float32)
    return jnp.stack([real, imag]).astype(jnp.bfloat16)


def on_device_plain(field, cotangent, mode_weight, skip_weight, lift_weight, proj_weight):
    chans, xrows, yrows, zlen = field.shape
    groups_x = lax.axis_size("gx")
    groups_y = lax.axis_size("gy")
    groups_c = lax.axis_size("col")
    span_x = xrows * groups_x
    span_y = yrows * groups_y * groups_c
    column = jnp.arange(MZ, dtype=jnp.int32)
    z_table = real_table(column, zlen)
    y_table = complex_table(centered(MY), span_y)
    x_table = complex_table(centered(MX), span_x).reshape(2, groups_x, xrows, 2, MX)
    tables = (z_table, y_table, x_table)
    local_modes = (mode_weight.shape[3], mode_weight.shape[4], mode_weight.shape[5])
    weight_flat = mode_weight.reshape(2, chans, chans, -1)
    modes = to_modes(field, tables)
    spectral = to_grid(mix(weight_flat, modes), tables, field.shape, local_modes).reshape(chans, -1)
    flat_field = field.reshape(chans, -1)
    flat_grad = cotangent.reshape(chans, -1)
    pre = spectral + jnp.dot(skip_weight, flat_field, preferred_element_type=jnp.float32)
    lifted, slope_pre = gelu_slope(pre)
    lifted = lifted.astype(jnp.bfloat16)
    hidden = jnp.dot(lift_weight, lifted, preferred_element_type=jnp.float32)
    activated, slope_hid = gelu_slope(hidden)
    activated = activated.astype(jnp.bfloat16)
    back_hidden = jnp.dot(proj_weight.T, flat_grad, preferred_element_type=jnp.float32)
    hidden_grad = (back_hidden * slope_hid).astype(jnp.bfloat16)
    grad_up = flat_grad.astype(jnp.float32) + jnp.dot(
        lift_weight.T, hidden_grad, preferred_element_type=jnp.float32
    )
    pre_grad = (grad_up * slope_pre).astype(jnp.bfloat16)
    proj_part = jnp.einsum("cr,hr->ch", flat_grad, activated, preferred_element_type=jnp.float32)
    lift_part = jnp.einsum("hr,cr->hc", hidden_grad, lifted, preferred_element_type=jnp.float32)
    skip_part = jnp.einsum("or,ir->oi", pre_grad, flat_field, preferred_element_type=jnp.float32)
    proj_grad, lift_grad, skip_grad = lax.psum(
        (proj_part, lift_part, skip_part), ("gx", "gy", "col")
    )
    pre_modes = to_modes(pre_grad.reshape(field.shape), tables)
    grad_real = jnp.einsum("ik,ok->iok", modes[0], pre_modes[0], preferred_element_type=jnp.float32)
    grad_real = grad_real + jnp.einsum(
        "ik,ok->iok", modes[1], pre_modes[1], preferred_element_type=jnp.float32
    )
    grad_imag = jnp.einsum("ik,ok->iok", modes[0], pre_modes[1], preferred_element_type=jnp.float32)
    grad_imag = grad_imag - jnp.einsum(
        "ik,ok->iok", modes[1], pre_modes[0], preferred_element_type=jnp.float32
    )
    mode_grad = jnp.stack([grad_real, grad_imag]).astype(jnp.bfloat16).reshape(mode_weight.shape)
    back_real = jnp.einsum(
        "iok,ok->ik", weight_flat[0], pre_modes[0], preferred_element_type=jnp.float32
    )
    back_real = back_real + jnp.einsum(
        "iok,ok->ik", weight_flat[1], pre_modes[1], preferred_element_type=jnp.float32
    )
    back_imag = jnp.einsum(
        "iok,ok->ik", weight_flat[0], pre_modes[1], preferred_element_type=jnp.float32
    )
    back_imag = back_imag - jnp.einsum(
        "iok,ok->ik", weight_flat[1], pre_modes[0], preferred_element_type=jnp.float32
    )
    modes_grad = jnp.stack([back_real, back_imag]).astype(jnp.bfloat16)
    spectral_grad = to_grid(modes_grad, tables, field.shape, local_modes).reshape(chans, -1)
    skip_back = jnp.dot(skip_weight.T, pre_grad, preferred_element_type=jnp.float32)
    field_grad = (spectral_grad + skip_back).astype(jnp.bfloat16).reshape(field.shape)
    return (field_grad, mode_grad, skip_grad, lift_grad, proj_grad)


F32 = jnp.float32
BF16 = jnp.bfloat16
LANES = 128


def np_trig(freqs, length):
    turns = (np.arange(length)[:, None] * (freqs[None, :] % length)) % length
    angle = turns.astype(np.float32) * np.float32(2.0 * math.pi / length)
    factor = np.float32(1.0 / math.sqrt(length))
    return (np.cos(angle) * factor, np.sin(angle) * factor)


def np_complex(freqs, length):
    cosine, sine = np_trig(freqs, length)
    upper = np.stack([cosine, -sine], axis=1)
    lower = np.stack([sine, cosine], axis=1)
    return np.stack([upper, lower])


def host_tables(zlen, yrows, xrows, n_z, n_y, half):
    cosine, sine = np_trig(np.arange(MZ), zlen)
    z_pair = np.stack([cosine.T, -sine.T], axis=1).reshape(2 * MZ, zlen)
    y_full = np_complex(np.arange(MY) - MY // 2, yrows * n_z)
    kyb = MY // n_y
    y_six = y_full.reshape(2, n_z, yrows, 2, n_y, kyb)
    y_fwd = y_six.transpose(4, 3, 5, 1, 0, 2).reshape(2 * MY, 2 * yrows * n_z)
    y_inv = y_six.transpose(1, 0, 2, 4, 3, 5).reshape(2 * yrows * n_z, 2 * MY)
    x_full = np_complex(np.arange(MX) - MX // 2, xrows * n_y).reshape(2, n_y, xrows, 2, MX)
    x_rows = x_full.transpose(1, 0, 2, 3, 4).reshape(n_y, 2, xrows, 1, 2 * MX)
    x_rows = np.broadcast_to(x_rows, (n_y, 2, xrows, half, 2 * MX)).reshape(-1, 2 * MX)
    x_fwd = np.concatenate([x_rows, x_rows], axis=1)
    x_cols = x_full.transpose(3, 4, 1, 0, 2).reshape(2 * MX, n_y, 2, xrows, 1)
    x_inv = np.broadcast_to(x_cols, (2 * MX, n_y, 2, xrows, half)).reshape(2 * MX, -1)
    return [
        jnp.asarray(np.ascontiguousarray(table), BF16)
        for table in (z_pair, y_fwd, y_inv, x_fwd, x_inv)
    ]


def dot(left, right, dims=((1,), (0,))):
    return lax.dot_general(left, right, (dims, ((), ())), preferred_element_type=F32)


NT = ((1,), (1,))
TN = ((0,), (0,))


def gelu_pair(value):
    square = value * value
    tangent = jnp.tanh(value * (KAPPA + (KAPPA * CUBIC) * square))
    half = 0.5 + 0.5 * tangent
    result = value * half
    slope = half + result * (1.0 - tangent) * (KAPPA + (3.0 * KAPPA * CUBIC) * square)
    return (result, slope)


def layer_kernel(
    geo, field_ref, cot_ref, weight_ref, skip_ref, lift_ref, proj_ref,
    tz_ref, tyf_ref, tyi_ref, txf_ref, txi_ref,
    grad_ref, modes_out, premodes_out, sums_out,
    held, packed, dense, cells, cots, cot_in, pgrad, kxf, kxi, spec_grid, mixed, spread,
    modes_ref, premodes_ref, up, send_z, recv_z, send_y, recv_y, sums, sums_x, sums_z,
    weight_sem, own_sem, send_sem, recv_sem, io_sem,
):
    n_gy, n_col, n_y, chans, xrows, yrows, kzb, kyb = geo
    n_z = n_gy * n_col
    half = LANES // xrows
    parts = chans // half
    zlen = cells.shape[-1]
    my_gy, my_col, my_gx = lax.axis_index("gy"), lax.axis_index("col"), lax.axis_index("gx")
    me_z, me_y = my_gy * n_col + my_col, my_gx

    folds = LANES // MX
    fold_rows = kzb * kyb // folds
    loads = weight_sem.shape[0]
    load_chans = chans // loads

    def weight_load(index):
        span = pl.ds(index * load_chans, load_chans)
        return pltpu.make_async_copy(
            weight_ref.at[:, span], held.at[:, span], weight_sem.at[index]
        )

    cot_load = pltpu.make_async_copy(cot_ref, cot_in, io_sem.at[0])
    cot_load.start()
    def load_ahead(first, last):
        for index in range(first, min(last, loads)):
            weight_load(index).start()

    load_ahead(0, 2)

    def fold(tall):
        return jnp.concatenate(
            [tall[at * fold_rows:(at + 1) * fold_rows] for at in range(folds)], axis=1
        )

    block_of = lax.broadcasted_iota(jnp.int32, (fold_rows, LANES), 1) // MX

    def shifts(tiles):
        return [
            [tile] + [pltpu.roll(tile, step * MX, 1) for step in range(1, folds)] for tile in tiles
        ]

    def swap_blocks(moved):
        swapped = []
        for lane in range(folds):
            total = moved[0][-lane % folds]
            for row in range(1, folds):
                total = jnp.where(block_of == row, moved[row][(row - lane) % folds], total)
            swapped.append(total)
        return swapped

    def pack_weight(index):
        weight_load(index).wait()
        outs = 8

        def body(block, carry):
            first = block * outs
            for chan in range(index * load_chans, (index + 1) * load_chans):
                for piece in range(2):
                    for out in range(outs):
                        packed[piece, chan, first + out] = fold(held[piece, chan, first + out])
            return carry

        lax.fori_loop(0, chans // outs, body, 0)

    def peer_z(step):
        other = lax.rem(me_z + step, n_z)
        return other, {"gy": other // n_col, "col": lax.rem(other, n_col)}

    def peer_y(step):
        other = lax.rem(me_y + step, n_y)
        return other, {"gx": other}

    barrier = pltpu.get_barrier_semaphore()
    for step in range(1, n_z):
        pl.semaphore_signal(
            barrier, inc=1, device_id=peer_z(step)[1], device_id_type=pl.DeviceIdType.MESH
        )
    for step in range(1, n_y):
        pl.semaphore_signal(
            barrier, inc=1, device_id=peer_y(step)[1], device_id_type=pl.DeviceIdType.MESH
        )

    def exchange(slot, send, recv, count, me, peer):
        copies = []
        for step in range(1, count):
            other, where = peer(step)
            copy = pltpu.make_async_remote_copy(
                src_ref=send.at[other],
                dst_ref=recv.at[me],
                send_sem=send_sem.at[slot, step],
                recv_sem=recv_sem.at[slot, step],
                device_id=where,
                device_id_type=pl.DeviceIdType.MESH,
            )
            copy.start()
            copies.append(copy)
        own = pltpu.make_async_copy(send.at[me], recv.at[me], own_sem.at[slot])
        own.start()
        copies.append(own)
        return copies

    def exchange_z(phase, part):
        return exchange(
            2 * phase * parts + part, send_z.at[part], recv_z.at[phase, part],
            n_z, me_z, peer_z,
        )

    def exchange_y(phase, part):
        return exchange(
            (2 * phase + 1) * parts + part, send_y.at[part], recv_y.at[phase, part],
            n_y, me_y, peer_y,
        )

    def finish(copies):
        for copy in copies:
            copy.wait()

    def cells_first(source, target):
        for cell in range(xrows):
            rows = source[:, cell, :, :].astype(F32)
            target[:, cell] = jnp.transpose(rows, (1, 0, 2)).astype(BF16)

    def chans_of(part):
        return slice(part * half, (part + 1) * half)

    def start_z(source, phase, part):
        planes = [
            dot(tz_ref[...], source[row, :, chans_of(part), :].reshape(LANES, zlen), NT)
            for row in range(yrows)
        ]
        turned = jnp.transpose(jnp.stack(planes), (1, 0, 2))
        turned = turned.reshape(n_z, kzb, 2 * yrows, LANES).astype(BF16)
        for block in range(n_z):
            send_z[part, block] = jnp.concatenate(
                [turned[block, freq] for freq in range(kzb)], axis=1
            )
        return exchange_z(phase, part)

    def start_y(phase, part):
        rows = recv_z[phase, part].reshape(n_z * 2 * yrows, kzb * LANES)
        moved = dot(tyf_ref[...], rows).astype(BF16)
        send_y[part] = moved.reshape(n_y, 2 * kyb, kzb * LANES)
        return exchange_y(phase, part)

    def reach_modes(phase, part, target):
        blocks = [recv_y[phase, part, group].astype(F32) for group in range(n_y)]
        columns = []
        for group in range(n_y):
            for piece in range(2):
                tiles = [
                    blocks[group][
                        piece * kyb:(piece + 1) * kyb, freq * LANES:(freq + 1) * LANES
                    ]
                    for freq in range(kzb)
                ]
                columns.append(jnp.concatenate(tiles, axis=0).astype(BF16))
        result = dot(jnp.concatenate(columns, axis=1), kxf[...])
        for tile in range(half * 2 * MX // LANES):
            tiles = [
                result[row * fold_rows:(row + 1) * fold_rows, tile * LANES:(tile + 1) * LANES]
                for row in range(folds)
            ]
            moved = shifts(tiles)
            swapped = swap_blocks(moved)
            for lane in range(folds):
                chan, piece = divmod(tile * folds + lane, 2)
                dense[piece, part * half + chan] = swapped[lane].astype(BF16)
                for row in range(folds):
                    target[
                        piece, part * half + chan, row * fold_rows:(row + 1) * fold_rows, :
                    ] = moved[row][-lane % folds][:, :MX].astype(BF16)

    run = 4

    def mix(summed_part, out_part):
        def body(index, carry):
            at = summed_part * half + index * run
            real = [dense[0, at + step] for step in range(run)]
            imag = [dense[1, at + step] for step in range(run)]
            for out in range(out_part * half, (out_part + 1) * half):
                short = [None, None]
                for step in range(run):
                    w_real, w_imag = packed[0, at + step, out], packed[1, at + step, out]
                    new = (
                        w_real * real[step] - w_imag * imag[step],
                        w_real * imag[step] + w_imag * real[step],
                    )
                    for piece in range(2):
                        old = short[piece]
                        short[piece] = new[piece] if old is None else old + new[piece]
                for piece in range(2):
                    mixed[piece, out] += short[piece].astype(F32)
            return carry

        lax.fori_loop(0, half // run, body, 0)

    def mix_back(summed_part, out_part):
        outs = 4

        def body(index, carry):
            first = out_part * half + index * outs
            total = [[mixed[piece, first + out] for piece in range(2)] for out in range(outs)]
            short = [[None, None] for _ in range(outs)]
            for step in range(half):
                summed = summed_part * half + step
                real, imag = dense[0, summed], dense[1, summed]
                for out in range(outs):
                    w_real, w_imag = packed[0, first + out, summed], packed[1, first + out, summed]
                    new = (w_real * real + w_imag * imag, w_real * imag - w_imag * real)
                    for piece in range(2):
                        old = short[out][piece]
                        short[out][piece] = new[piece] if old is None else old + new[piece]
                        if (step + 1) % run == 0:
                            total[out][piece] = total[out][piece] + short[out][piece].astype(F32)
                            short[out][piece] = None
            for out in range(outs):
                for piece in range(2):
                    mixed[piece, first + out] = total[out][piece]
            return carry

        lax.fori_loop(0, half // outs, body, 0)

    def start_back_x(phase, part):
        for tile in range(half * 2 * MX // LANES):
            tiles = []
            for lane in range(folds):
                chan, piece = divmod(tile * folds + lane, 2)
                tiles.append(mixed[piece, part * half + chan])
            swapped = swap_blocks(shifts(tiles))
            for row in range(folds):
                spread[
                    part, row * fold_rows:(row + 1) * fold_rows, tile * LANES:(tile + 1) * LANES
                ] = swapped[row].astype(BF16)
        both = dot(spread[part], kxi[...])
        for group in range(n_y):
            rows = []
            for piece in range(2):
                at = (group * 2 + piece) * LANES
                rows.append(jnp.concatenate(
                    [both[freq * kyb:(freq + 1) * kyb, at:at + LANES] for freq in range(kzb)],
                    axis=1,
                ))
            send_y[part, group] = jnp.concatenate(rows, axis=0).astype(BF16)
        return exchange_y(phase, part)

    def start_back_y(phase, part):
        rows = recv_y[phase, part].reshape(n_y * 2 * kyb, kzb * LANES)
        moved = dot(tyi_ref[...], rows).astype(BF16)
        send_z[part] = moved.reshape(n_z, 2 * yrows, kzb * LANES)
        return exchange_z(phase, part)

    def reach_grid(phase, part, emit):
        tiles = []
        for block in range(n_z):
            rows = recv_z[phase, part, block].astype(F32)
            for freq in range(kzb):
                for piece in range(2):
                    tiles.append(
                        rows[piece * yrows:(piece + 1) * yrows, freq * LANES:(freq + 1) * LANES]
                    )
        turned = jnp.transpose(jnp.stack(tiles), (1, 0, 2)).astype(BF16)
        for row in range(yrows):
            emit(row, part, dot(turned[row], tz_ref[...], TN).reshape(xrows, half, zlen))

    def keep_grid(row, part, values):
        spec_grid[row, :, chans_of(part), :] += values

    def keep_grad(row, part, values):
        total = values + spec_grid[row, :, chans_of(part), :]
        grad_ref[row, :, chans_of(part), :] = total.astype(BF16)

    def wide_cells(ref, row):
        return jnp.concatenate([ref[row, cell] for cell in range(xrows)], axis=1)

    def build_x_tables():
        tall, wide = kxf.shape
        lane = lax.broadcasted_iota(jnp.int32, (tall, LANES), 1)
        line = lax.broadcasted_iota(jnp.int32, (tall, LANES), 0)
        owner = line % half
        pair = txf_ref[...].astype(F32)
        per_tile = LANES // (2 * MX)
        for tile in range(wide // LANES):
            keep = owner == tile * per_tile + lane // (2 * MX)
            kxf[:, tile * LANES:(tile + 1) * LANES] = jnp.where(keep, pair, 0.0).astype(BF16)
        flat = txi_ref[...].astype(F32)
        lane_owner = lax.broadcasted_iota(jnp.int32, flat.shape, 1) % half
        for chan in range(half):
            kxi[chan * 2 * MX:(chan + 1) * 2 * MX, :] = jnp.where(
                lane_owner == chan, flat, 0.0
            ).astype(BF16)

    def prepare(row, carry):
        up[row] = dot(proj_ref[...], wide_cells(cots, row), TN).astype(BF16)
        total = dot(skip_ref[...], wide_cells(cells, row))
        for cell in range(xrows):
            spec_grid[row, cell] = total[:, cell * zlen:(cell + 1) * zlen]
        return carry

    both = range(parts)
    clear = jnp.zeros(mixed.shape, F32)
    cells_first(field_ref, cells)
    load_ahead(2, 4)
    build_x_tables()
    mixed[...] = clear
    pl.semaphore_wait(barrier, n_z - 1 + n_y - 1)
    going_z = [start_z(cells, 0, part) for part in both]
    load_ahead(4, 6)
    early = 3 * loads // 8
    for index in range(early):
        pack_weight(index)
        load_ahead(6 + index, 7 + index)
    going_y = []
    for part in both:
        finish(going_z[part])
        going_y.append(start_y(0, part))
        if part < parts - 1:
            pack_weight(early + part)
    for index in range(early + parts - 1, loads):
        pack_weight(index)
    for part in both:
        finish(going_y[part])
        reach_modes(0, part, modes_ref)
        if part < parts - 1:
            for out_part in both:
                mix(part, out_part)
    modes_save = pltpu.make_async_copy(modes_ref, modes_out, io_sem.at[1])
    modes_save.start()
    going_y = []
    for part in both:
        mix(parts - 1, part)
        going_y.append(start_back_x(1, part))
    cot_load.wait()
    cells_first(cot_in, cots)
    lax.fori_loop(0, yrows, prepare, 0)
    going_z = []
    for part in both:
        finish(going_y[part])
        going_z.append(start_back_y(1, part))
    sums[...] = jnp.zeros(sums.shape, F32)
    mixed[...] = clear
    for part in both:
        finish(going_z[part])
        reach_grid(1, part, keep_grid)

    pair = 2

    def pointwise(step, carry):
        lines = [step * pair + line for line in range(pair)]
        grads = jnp.concatenate([wide_cells(cots, row) for row in lines], axis=1)
        pre = jnp.concatenate(
            [spec_grid[row, cell] for row in lines for cell in range(xrows)], axis=1
        )
        lifted, slope_pre = gelu_pair(pre)
        lifted = lifted.astype(BF16)
        hidden = dot(lift_ref[...], lifted, TN)
        activated, slope_hid = gelu_pair(hidden)
        activated = activated.astype(BF16)
        above = jnp.concatenate([up[row] for row in lines], axis=1).astype(F32)
        hidden_grad = (above * slope_hid).astype(BF16)
        grad_up = grads.astype(F32) + dot(lift_ref[...], hidden_grad)
        pre_grad = (grad_up * slope_pre).astype(BF16)
        sums[0:chans] += dot(grads, activated, NT)
        for line in range(pair):
            span = xrows * zlen
            up[lines[line]] = hidden_grad[:, line * span:(line + 1) * span]
            for cell in range(xrows):
                at = (line * xrows + cell) * zlen
                pgrad[lines[line], cell] = pre_grad[:, at:at + zlen]
                spec_grid[lines[line], cell] = lifted[:, at:at + zlen].astype(F32)
        return carry

    def late_sums(row, carry):
        lifted = wide_cells(spec_grid, row).astype(BF16)
        sums[chans:2 * chans] += dot(lifted, up[row], NT)
        sums[2 * chans:, 0:chans] += dot(wide_cells(pgrad, row), wide_cells(cells, row), NT)
        return carry

    lax.fori_loop(0, yrows // pair, pointwise, 0)

    share = sums.shape[0] // n_y
    spare = 8 * parts

    def send_sums(slot, count, me, peer, source, target):
        copies = []
        for step in range(1, count):
            other, where = peer(step)
            copy = pltpu.make_async_remote_copy(
                src_ref=source(other),
                dst_ref=target.at[me],
                send_sem=send_sem.at[slot, step],
                recv_sem=recv_sem.at[slot, step],
                device_id=where,
                device_id_type=pl.DeviceIdType.MESH,
            )
            copy.start()
            copies.append(copy)
        return copies

    def rows_of(index):
        return pl.ds(pl.multiple_of(index * share, 8), share)

    def skip_back(row, carry):
        total = dot(skip_ref[...], wide_cells(pgrad, row), TN)
        for cell in range(xrows):
            spec_grid[row, cell] = total[:, cell * zlen:(cell + 1) * zlen]
        return carry

    going_z = [start_z(pgrad, 2, part) for part in both]
    lax.fori_loop(0, yrows, late_sums, 0)
    sums_x[me_y] = sums[rows_of(me_y), :]
    small = send_sums(spare, n_y, me_y, peer_y, lambda other: sums.at[rows_of(other)], sums_x)
    going_y = []
    for part in both:
        finish(going_z[part])
        going_y.append(start_y(2, part))
    lax.fori_loop(0, yrows, skip_back, 0)
    for part in both:
        finish(going_y[part])
        reach_modes(2, part, premodes_ref)
        if part < parts - 1:
            for out_part in both:
                mix_back(part, out_part)
        if part == 0:
            finish(small)
            sums_z[me_z] = jnp.sum(sums_x[...], axis=0)
            small = send_sums(
                spare + 1, n_z, me_z, peer_z, lambda other: sums_z.at[me_z], sums_z
            )
    premodes_save = pltpu.make_async_copy(premodes_ref, premodes_out, io_sem.at[2])
    premodes_save.start()
    going_y = []
    for part in both:
        mix_back(parts - 1, part)
        going_y.append(start_back_x(3, part))
    finish(small)
    sums_out[me_y] = jnp.sum(sums_z[...], axis=0)
    small = send_sums(spare + 2, n_y, me_y, peer_y, lambda other: sums_out.at[me_y], sums_out)
    going_z = []
    for part in both:
        finish(going_y[part])
        going_z.append(start_back_y(3, part))
    finish(small)
    modes_save.wait()
    premodes_save.wait()
    for part in both:
        finish(going_z[part])
        reach_grid(3, part, keep_grad)


def outer_kernel(
    modes_ref, pre_ref, grid_ref, sums_ref, out_ref, field_ref, proj_ref, lift_ref, skip_ref,
    held, grid, turned, out_sem, io_sem,
):
    chans, rows = pre_ref.shape[1], pre_ref.shape[2]
    count = out_sem.shape[0]
    group = chans // count

    grid_load = pltpu.make_async_copy(grid_ref, grid, io_sem.at[0])
    grid_load.start()

    def save(index):
        span = pl.ds(index * group, group)
        return pltpu.make_async_copy(held.at[:, span], out_ref.at[:, span], out_sem.at[index])

    def outer(index, carry):
        first = index * group
        outs = 4

        def body(block, inner):
            for top in range(0, rows, 16):
                m_real = [modes_ref[0, first + chan, top:top + 16] for chan in range(group)]
                m_imag = [modes_ref[1, first + chan, top:top + 16] for chan in range(group)]
                for step in range(outs):
                    out = block * outs + step
                    p_real, p_imag = pre_ref[0, out, top:top + 16], pre_ref[1, out, top:top + 16]
                    for chan in range(group):
                        real = m_real[chan] * p_real + m_imag[chan] * p_imag
                        imag = m_real[chan] * p_imag - m_imag[chan] * p_real
                        held[0, first + chan, out, top:top + 16] = real
                        held[1, first + chan, out, top:top + 16] = imag
            return inner

        lax.fori_loop(0, chans // outs, body, 0)
        save(index).start()
        return carry

    lax.fori_loop(0, count, outer, 0)
    grid_load.wait()
    for cell in range(grid.shape[1]):
        turned[:, cell] = jnp.transpose(grid[:, cell].astype(F32), (1, 0, 2)).astype(BF16)
    field_save = pltpu.make_async_copy(turned, field_ref, io_sem.at[1])
    field_save.start()
    proj_ref[...] = sums_ref[0:chans]
    lift_ref[...] = sums_ref[chans:2 * chans]
    skip_ref[...] = sums_ref[2 * chans:, 0:chans]

    def done(index, carry):
        save(index).wait()
        return carry

    lax.fori_loop(0, count, done, 0)
    field_save.wait()


def finish_gradients(modes, pre_modes, grid, sums):
    _, chans, rows, lanes = modes.shape
    yrows, xrows, _, zlen = grid.shape
    whole = (2, chans, chans, rows, lanes)
    field_shape = (chans, xrows, yrows, zlen)
    vmem = pl.BlockSpec(memory_space=pltpu.VMEM)
    hbm = pl.BlockSpec(memory_space=pl.ANY)
    return pl.pallas_call(
        outer_kernel,
        in_specs=[vmem, vmem, hbm, vmem],
        out_specs=[hbm, hbm, vmem, vmem, vmem],
        out_shape=(
            jax.ShapeDtypeStruct(whole, BF16),
            jax.ShapeDtypeStruct(field_shape, BF16),
            jax.ShapeDtypeStruct((chans, LANES), F32),
            jax.ShapeDtypeStruct((chans, LANES), F32),
            jax.ShapeDtypeStruct((chans, chans), F32),
        ),
        scratch_shapes=[
            pltpu.VMEM(whole, BF16),
            pltpu.VMEM(grid.shape, BF16),
            pltpu.VMEM(field_shape, BF16),
            pltpu.SemaphoreType.DMA((chans // 2,)),
            pltpu.SemaphoreType.DMA((2,)),
        ],
        compiler_params=pltpu.CompilerParams(vmem_limit_bytes=60 << 20),
        name="mode_outer",
    )(modes, pre_modes, grid, sums)


def on_device(field, cotangent, mode_weight, skip_weight, lift_weight, proj_weight):
    chans, xrows, yrows, zlen = field.shape
    kzb, kyb = mode_weight.shape[3], mode_weight.shape[4]
    n_gy, n_col, n_y = lax.axis_size("gy"), lax.axis_size("col"), lax.axis_size("gx")
    n_z = n_gy * n_col
    fits = kyb == 8 and kzb % 2 == 0 and xrows == 8 and yrows == 8 and zlen == LANES
    fits = fits and lift_weight.shape[0] == LANES and (3 * chans) % (8 * n_y) == 0 and chans % 8 == 0
    fits = fits and (kzb * kyb * MX) % (16 * LANES) == 0
    if not fits or 2 * MX * 2 != LANES or chans % (LANES // xrows) or LANES // xrows != 16:
        return on_device_plain(
            field, cotangent, mode_weight, skip_weight, lift_weight, proj_weight
        )
    half = LANES // xrows
    parts = chans // half
    rows = kzb * kyb
    tables = host_tables(zlen, yrows, xrows, n_z, n_y, half)
    weight = mode_weight.reshape(2, chans, chans, rows, MX)
    share = 3 * chans // n_y
    vmem = pl.BlockSpec(memory_space=pltpu.VMEM)
    hbm = pl.BlockSpec(memory_space=pl.ANY)
    geo = (n_gy, n_col, n_y, chans, xrows, yrows, kzb, kyb)
    grid_shape = (yrows, xrows, chans, zlen)
    spectral = (2, chans, rows, MX)
    packed = (2, chans, rows * MX // LANES, LANES)
    outs = pl.pallas_call(
        functools.partial(layer_kernel, geo),
        out_shape=(
            jax.ShapeDtypeStruct(grid_shape, BF16),
            jax.ShapeDtypeStruct(spectral, BF16),
            jax.ShapeDtypeStruct(spectral, BF16),
            jax.ShapeDtypeStruct((n_y, share, LANES), F32),
        ),
        in_specs=[vmem, hbm, hbm] + [vmem] * 8,
        out_specs=(vmem, hbm, hbm, vmem),
        scratch_shapes=[
            pltpu.VMEM(weight.shape, BF16),
            pltpu.VMEM((2, chans, chans, rows * MX // LANES, LANES), BF16),
            pltpu.VMEM(packed, BF16),
            pltpu.VMEM(grid_shape, BF16),
            pltpu.VMEM(grid_shape, BF16),
            pltpu.VMEM(cotangent.shape, BF16),
            pltpu.VMEM(grid_shape, BF16),
            pltpu.VMEM((n_y * 2 * LANES, half * 2 * MX), BF16),
            pltpu.VMEM((half * 2 * MX, n_y * 2 * LANES), BF16),
            pltpu.VMEM(grid_shape, F32),
            pltpu.VMEM(packed, F32),
            pltpu.VMEM((parts, rows, half * 2 * MX), BF16),
            pltpu.VMEM(spectral, BF16),
            pltpu.VMEM(spectral, BF16),
            pltpu.VMEM((yrows, lift_weight.shape[0], xrows * zlen), BF16),
            pltpu.VMEM((parts, n_z, 2 * yrows, kzb * LANES), BF16),
            pltpu.VMEM((4, parts, n_z, 2 * yrows, kzb * LANES), BF16),
            pltpu.VMEM((parts, n_y, 2 * kyb, kzb * LANES), BF16),
            pltpu.VMEM((4, parts, n_y, 2 * kyb, kzb * LANES), BF16),
            pltpu.VMEM((n_y * share, LANES), F32),
            pltpu.VMEM((n_y, share, LANES), F32),
            pltpu.VMEM((n_z, share, LANES), F32),
            pltpu.SemaphoreType.DMA((8,)),
            pltpu.SemaphoreType.DMA((8 * parts,)),
            pltpu.SemaphoreType.DMA((8 * parts + 3, max(n_z, n_y))),
            pltpu.SemaphoreType.DMA((8 * parts + 3, max(n_z, n_y))),
            pltpu.SemaphoreType.DMA((3,)),
        ],
        compiler_params=pltpu.CompilerParams(
            collective_id=0, has_side_effects=True, vmem_limit_bytes=62 << 20
        ),
        name="spectral_layer",
    )(field, cotangent, weight, skip_weight, lift_weight.T, proj_weight, *tables)
    grad, modes, pre_modes, sums = outs
    mode_grad, field_grad, proj_grad, lift_turned, skip_grad = finish_gradients(
        modes, pre_modes, grad, sums.reshape(3 * chans, LANES)
    )
    return (field_grad, mode_grad.reshape(mode_weight.shape), skip_grad, lift_turned.T, proj_grad)


def solution(mesh):
    in_specs = (
        P("grp", "gx", ("gy", "col"), None),
        P("grp", "gx", ("gy", "col"), None),
        P(None, None, None, ("gy", "col"), "gx", None),
        P(),
        P(),
        P(),
    )
    out_specs = (
        P("grp", "gx", ("gy", "col"), None),
        P("grp", None, None, ("gy", "col"), "gx", None),
        P("grp", None),
        P("grp", None),
        P("grp", None),
    )
    return jax.shard_map(
        on_device, mesh=mesh, in_specs=in_specs, out_specs=out_specs, check_vma=False
    )
```
